32 devices in a mesh: dp: 8 (over y, x, core), tensor: 4 (over z).
Axes of the slice: x: 2, y: 2, z: 4, core: 2. Of those that a mesh axis runs over, the one named last changes fastest.
Arguments:
- tokens: bfloat16 [16, 577, 1024], P('dp', None, 'tensor'), may hold values from -6 to 6
- cotangent: float32 [16, 577, 1024], P('dp', None, 'tensor'), may hold values from -6 to 6
- image_counts: int32 [8], P('dp'), may hold values from 1 to 2, as said below
- w_qkv: float32 [2, 1024, 3, 1024], P(None, 'dp', None, 'tensor'), as said below
- w_out: float32 [2, 1024, 1024], P(None, 'dp', 'tensor'), may hold values from -0.75 to 0.75
- w_fc1: float32 [2, 1024, 4096], P(None, 'dp', 'tensor'), may hold values from -0.1875 to 0.1875
- w_fc2: float32 [2, 1024, 4096], P(None, 'dp', 'tensor'), may hold values from -0.09375 to 0.09375
- vec_small: float32 [2, 8, 1024], P(None, None, 'tensor'), as said below
- fc1_bias: float32 [2, 4096], P(None, 'tensor'), may hold values from -3 to 3
- mom_qkv: float32 [2, 2, 1024, 3, 1024], P(None, None, 'dp', None, 'tensor'), as said below
- mom_out: float32 [2, 2, 1024, 1024], P(None, None, 'dp', 'tensor'), as said below
- mom_fc1: float32 [2, 2, 1024, 4096], P(None, None, 'dp', 'tensor'), as said below
- mom_fc2: float32 [2, 2, 1024, 4096], P(None, None, 'dp', 'tensor'), as said below
- mom_vec: float32 [2, 2, 8, 1024], P(None, None, None, 'tensor'), as said below
- mom_bias: float32 [2, 2, 4096], P(None, None, 'tensor'), as said below
Outputs:
- output: float32 [16, 577, 1024], P('dp', None, 'tensor')
- input_grad: float32 [16, 577, 1024], P('dp', None, 'tensor')
- grad_qkv: float32 [2, 1024, 3, 1024], P(None, 'dp', None, 'tensor')
- grad_out: float32 [2, 1024, 1024], P(None, 'dp', 'tensor')
- grad_fc1: float32 [2, 1024, 4096], P(None, 'dp', 'tensor')
- grad_fc2: float32 [2, 1024, 4096], P(None, 'dp', 'tensor')
- grad_vec: float32 [2, 8, 1024], P(None, None, 'tensor')
- grad_bias: float32 [2, 4096], P(None, 'tensor')
- new_qkv: float32 [2, 1024, 3, 1024], P(None, 'dp', None, 'tensor')
- new_out: float32 [2, 1024, 1024], P(None, 'dp', 'tensor')
- new_fc1: float32 [2, 1024, 4096], P(None, 'dp', 'tensor')
- new_fc2: float32 [2, 1024, 4096], P(None, 'dp', 'tensor')
- new_vec: float32 [2, 8, 1024], P(None, None, 'tensor')
- new_bias: float32 [2, 4096], P(None, 'tensor')
- newmom_qkv: float32 [2, 2, 1024, 3, 1024], P(None, None, 'dp', None, 'tensor')
- newmom_out: float32 [2, 2, 1024, 1024], P(None, None, 'dp', 'tensor')
- newmom_fc1: float32 [2, 2, 1024, 4096], P(None, None, 'dp', 'tensor')
- newmom_fc2: float32 [2, 2, 1024, 4096], P(None, None, 'dp', 'tensor')
- newmom_vec: float32 [2, 2, 8, 1024], P(None, None, None, 'tensor')
- newmom_bias: float32 [2, 2, 4096], P(None, None, 'tensor')
The draws below stay inside these ranges and needn't reach their ends.
Inputs may be any that keep to these rules, and one draw needn't show every extreme that they name: Every index of dp holds 1 or 2 images; some index holds 2 and some holds 1. Slot 2 i always holds an image, slot 2 i + 1 only where image_counts[i] is 2; other slots' tokens and cotangents are ignored. `w_qkv`: independent entries of mean 0 and deviation 1024^-0.5. `vec_small`: gains and shifts of order one. `mom_qkv`: second moments (index 1 of dimension 0) are positive. `mom_out`: second moments (index 1 of dimension 0) are positive. `mom_fc1`: second moments (index 1 of dimension 0) are positive. `mom_fc2`: second moments (index 1 of dimension 0) are positive. `mom_vec`: second moments (index 1 of dimension 0) are positive. `mom_bias`: second moments (index 1 of dimension 0) are positive.
All inputs are finite; a program needn't handle non-finite values.
Results may differ from the reference program's by a relative error of at most 0.022.
Values may be sent and summed in bfloat16 or wider, within the bound.
A program may use at most 256 MiB of HBM per device.

```python
import math
import jax
import jax.numpy as jnp
from jax import lax

D = 1024
HEADS = 16
FF = 4096
SEQ = 577
LAYERS = 2
STEP = 10
HD = 64
SLOTS = 16


def draw_image_counts(key, part):
    device_total = SLOTS // 2
    key_one, key_two, key_three = jax.random.split(key, 3)
    counts = jax.random.randint(key_one, (device_total,), 1, 3)
    busy_index = jax.random.randint(key_two, (), 0, device_total)
    light_index = (busy_index + 1 + jax.random.randint(key_three, (), 0, device_total - 1)) % device_total
    positions = jnp.arange(device_total)
    counts = jnp.where(positions == busy_index, 2, counts)
    counts = jnp.where(positions == light_index, 1, counts)
    return counts.astype(jnp.int32)


def draw_w_qkv(key, part):
    key_one = jax.random.fold_in(key, 0)
    base = jax.random.normal(key_one, (LAYERS, D, 3, D), jnp.float32) * D ** (-0.5)
    return base


def draw_vec_small(key, part):
    key_one, key_two = jax.random.split(key)
    raw_rows = jax.random.normal(key_one, (LAYERS, 8, D), jnp.float32) * 0.5
    gains = jnp.exp(jax.random.uniform(key_two, (LAYERS, 8, D), jnp.float32, -0.7, 0.7))
    row_index = jnp.arange(8)[None, :, None]
    return jnp.where((row_index == 0) | (row_index == 5), gains, raw_rows)


def second_level():
    return 0.0005 * (D / max(D // 16, 1)) * SLOTS * SEQ


def moment_pair(key, shape, level):
    key_one, key_two = jax.random.split(key)
    first = jax.random.normal(key_one, shape, jnp.float32) * 2.0
    second = level * jnp.exp(jax.random.uniform(key_two, shape, jnp.float32, math.log(0.3), math.log(3.0)))
    return jnp.stack([first, second])


def draw_mom_qkv(key, part):
    return moment_pair(jax.random.fold_in(key, 11), (LAYERS, D, 3, D), second_level())


def draw_mom_out(key, part):
    return moment_pair(jax.random.fold_in(key, 12), (LAYERS, D, D), 1.0)


def draw_mom_fc1(key, part):
    return moment_pair(jax.random.fold_in(key, 13), (LAYERS, D, FF), 1.0)


def draw_mom_fc2(key, part):
    return moment_pair(jax.random.fold_in(key, 14), (LAYERS, D, FF), 1.0)


def draw_mom_vec(key, part):
    return moment_pair(jax.random.fold_in(key, 15), (LAYERS, 8, D), second_level())


def draw_mom_bias(key, part):
    return moment_pair(jax.random.fold_in(key, 16), (LAYERS, FF), 1.0)


def shard_levels(key, extent, shards, low, high):
    def one(dim, shards_of):
        steps = jax.random.uniform(jax.random.fold_in(jax.random.fold_in(key, 6), dim), (shards_of,), jnp.float32, low / len(shards), high / len(shards))
        return jnp.repeat(jnp.exp(steps), extent[dim] // shards_of).reshape((-1,) + (1,) * (len(extent) - dim - 1))

    level = one(*shards[0])
    for cut in shards[1:]:
        level = level * one(*cut)
    return level


def centred(rng, dims, width, limit, pieces=(), dtype=jnp.bfloat16):
    entries = jax.random.normal(rng, dims, jnp.float32) * width
    if len(pieces) > 0:
        entries = shard_levels(rng, dims, pieces, -0.22, 0.18) * entries
    return jnp.clip(entries, min=-limit, max=limit).astype(dtype)


def setup_inputs(seed: int = 0) -> dict:
    arg_keys = jax.random.split(jax.random.key(seed), 16)
    tokens = centred(arg_keys[0], (SLOTS, SEQ, D), 1.0, 6.0, ((0, 8), (2, 4)))
    cotangent = centred(arg_keys[1], (SLOTS, SEQ, D), 1.0, 6.0, ((0, 8), (2, 4)), jnp.float32)
    image_counts = draw_image_counts(jax.random.fold_in(arg_keys[15], 71), 0)
    w_qkv = draw_w_qkv(jax.random.fold_in(arg_keys[15], 71), 0)
    w_out = centred(arg_keys[4], (LAYERS, D, D), (max(D // 16, 1)) ** -0.5, 0.75, ((1, 8), (2, 4)), jnp.float32)
    w_fc1 = centred(arg_keys[5], (LAYERS, D, FF), D ** -0.5, 0.1875, ((1, 8), (2, 4)), jnp.float32)
    w_fc2 = centred(arg_keys[6], (LAYERS, D, FF), FF ** -0.5, 0.09375, ((1, 8), (2, 4)), jnp.float32)
    vec_small = draw_vec_small(jax.random.fold_in(arg_keys[15], 71), 0)
    fc1_bias = centred(arg_keys[8], (LAYERS, FF), 0.5, 3.0, ((1, 4),), jnp.float32)
    mom_qkv = draw_mom_qkv(jax.random.fold_in(arg_keys[15], 71), 0)
    mom_out = draw_mom_out(jax.random.fold_in(arg_keys[15], 71), 0)
    mom_fc1 = draw_mom_fc1(jax.random.fold_in(arg_keys[15], 71), 0)
    mom_fc2 = draw_mom_fc2(jax.random.fold_in(arg_keys[15], 71), 0)
    mom_vec = draw_mom_vec(jax.random.fold_in(arg_keys[15], 71), 0)
    mom_bias = draw_mom_bias(jax.random.fold_in(arg_keys[15], 71), 0)
    return dict(tokens=tokens, cotangent=cotangent, image_counts=image_counts, w_qkv=w_qkv, w_out=w_out, w_fc1=w_fc1, w_fc2=w_fc2, vec_small=vec_small, fc1_bias=fc1_bias, mom_qkv=mom_qkv, mom_out=mom_out, mom_fc1=mom_fc1, mom_fc2=mom_fc2, mom_vec=mom_vec, mom_bias=mom_bias)


NORM_EPS = 1e-06
ROOT_HALF = 0.7071067811865476
INV_ROOT_TWO_PI = 0.3989422804014327
LEARN_RATE = 0.01
BETA_ONE = 0.9
BETA_TWO = 0.999
ADAM_EPS = 1e-08
WEIGHT_DECAY = 0.05

def gelu_value(preactivation):
    return 0.5 * preactivation * (1.0 + jax.scipy.special.erf(preactivation * ROOT_HALF))

def gelu_slope(preactivation):
    return 0.5 * (1.0 + jax.scipy.special.erf(preactivation * ROOT_HALF)) + preactivation * jnp.exp(-0.5 * preactivation * preactivation) * INV_ROOT_TWO_PI

def layernorm_forward(hidden_state):
    mean_row = lax.optimization_barrier(jnp.mean(hidden_state, -1, keepdims=True))
    spread = lax.optimization_barrier(jnp.mean(hidden_state * hidden_state, -1, keepdims=True)) - mean_row * mean_row
    inv_std = lax.rsqrt(spread + NORM_EPS)
    return ((hidden_state - mean_row) * inv_std, inv_std)

def layernorm_backward(d_normed, normed, inv_std, gain, carried):
    d_hat = d_normed * gain
    grad_in = carried + inv_std * (d_hat - lax.optimization_barrier(jnp.mean(d_hat, -1, keepdims=True)) - normed * lax.optimization_barrier(jnp.mean(d_hat * normed, -1, keepdims=True)))
    return (grad_in, lax.optimization_barrier(jnp.sum(d_normed * normed, 0)), lax.optimization_barrier(jnp.sum(d_normed, 0)))

def split_heads(matrix):
    return matrix.reshape(matrix.shape[0], HEADS, HD)

def attend_forward(query_h, key_h, value_h):
    scores = jnp.einsum('qhd,khd->hqk', query_h.astype(jnp.float32), key_h.astype(jnp.float32)) * HD ** (-0.5)
    top_score = lax.optimization_barrier(jnp.max(scores, -1, keepdims=True))
    logged_total = top_score + jnp.log(lax.optimization_barrier(jnp.sum(jnp.exp(scores - top_score), -1, keepdims=True)))
    probs = jnp.exp(scores - logged_total).astype(jnp.bfloat16)
    attention_result = jnp.einsum('hqk,khd->qhd', probs.astype(jnp.float32), value_h.astype(jnp.float32)).astype(jnp.bfloat16)
    return (attention_result, logged_total)

def attend_backward(query_h, key_h, value_h, attention_result, d_att, logged_total):
    scale_value = HD ** (-0.5)
    scores = jnp.einsum('qhd,khd->hqk', query_h.astype(jnp.float32), key_h.astype(jnp.float32)) * scale_value
    probs = jnp.exp(scores - logged_total)
    probs_low = probs.astype(jnp.bfloat16)
    d_value = jnp.einsum('hqk,qhd->khd', probs_low.astype(jnp.float32), d_att.astype(jnp.float32))
    d_probs = jnp.einsum('qhd,khd->hqk', d_att.astype(jnp.float32), value_h.astype(jnp.float32))
    delta = lax.optimization_barrier(jnp.sum(d_att.astype(jnp.float32) * attention_result.astype(jnp.float32), -1))
    d_scores = (probs * (d_probs - jnp.transpose(delta)[:, :, None]) * scale_value).astype(jnp.bfloat16)
    d_query = jnp.einsum('hqk,khd->qhd', d_scores.astype(jnp.float32), key_h.astype(jnp.float32))
    d_key = jnp.einsum('hqk,qhd->khd', d_scores.astype(jnp.float32), query_h.astype(jnp.float32))
    return (d_query, d_key, d_value)

def adam_update(param, running_gradient, moments, decay):
    first = BETA_ONE * moments[0] + (1.0 - BETA_ONE) * running_gradient
    second = BETA_TWO * moments[1] + (1.0 - BETA_TWO) * running_gradient * running_gradient
    fix_one = 1.0 - BETA_ONE ** STEP
    fix_two = 1.0 - BETA_TWO ** STEP
    update = first / fix_one / (jnp.sqrt(second / fix_two) + ADAM_EPS) + decay * param
    return (param - LEARN_RATE * update, jnp.stack([first, second]))

def reference(tokens, cotangent, image_counts, w_qkv, w_out, w_fc1, w_fc2, vec_small, fc1_bias, mom_qkv, mom_out, mom_fc1, mom_fc2, mom_vec, mom_bias):
    live_all = jnp.stack([jnp.ones_like(image_counts), (image_counts == 2).astype(jnp.int32)], 1).reshape(-1).astype(jnp.float32)

    def run_slot(totals, inputs):
        slot_tokens, slot_cot, slot_live = inputs
        hidden_state = slot_tokens.astype(jnp.float32)
        saved_tensors = []
        for layer_number in range(LAYERS):
            vector_rows = vec_small[layer_number]
            projection_weight = w_qkv[layer_number].astype(jnp.bfloat16).reshape(D, 3 * D)
            backward_weight = w_out[layer_number].astype(jnp.bfloat16)
            first_weight = w_fc1[layer_number].astype(jnp.bfloat16)
            second_weight = w_fc2[layer_number].astype(jnp.bfloat16)
            first_centered_scaled, first_inverse_deviation = layernorm_forward(hidden_state)
            first_normalized = (first_centered_scaled * vector_rows[0] + vector_rows[1]).astype(jnp.bfloat16)
            proj_out = jnp.dot(first_normalized, projection_weight, preferred_element_type=jnp.float32).reshape(SEQ, 3, D)
            query_matrix_rows = (proj_out[:, 0] + vector_rows[2]).astype(jnp.bfloat16)
            key_matrix_rows = proj_out[:, 1].astype(jnp.bfloat16)
            value_matrix_rows = (proj_out[:, 2] + vector_rows[3]).astype(jnp.bfloat16)
            attention_result, logged_total = attend_forward(split_heads(query_matrix_rows), split_heads(key_matrix_rows), split_heads(value_matrix_rows))
            attention_result = attention_result.reshape(SEQ, D)
            middle_state = hidden_state + jnp.dot(attention_result, backward_weight.T, preferred_element_type=jnp.float32) + vector_rows[4]
            second_centered_scaled, second_inverse_deviation = layernorm_forward(middle_state)
            second_normalized = (second_centered_scaled * vector_rows[5] + vector_rows[6]).astype(jnp.bfloat16)
            preactivation = jnp.dot(second_normalized, first_weight, preferred_element_type=jnp.float32) + fc1_bias[layer_number]
            activation_narrow = gelu_value(preactivation).astype(jnp.bfloat16)
            new_hidden = middle_state + jnp.dot(activation_narrow, second_weight.T, preferred_element_type=jnp.float32) + vector_rows[7]
            saved_tensors.append((projection_weight, backward_weight, first_weight, second_weight, first_centered_scaled, first_inverse_deviation, first_normalized, query_matrix_rows, key_matrix_rows, value_matrix_rows, attention_result, logged_total, second_centered_scaled, second_inverse_deviation, second_normalized, preactivation, activation_narrow))
            hidden_state = new_hidden
        running_gradient = slot_cot * slot_live
        layer_grads = [None] * LAYERS
        for layer_number in reversed(range(LAYERS)):
            vector_rows = vec_small[layer_number]
            projection_weight, backward_weight, first_weight, second_weight, first_centered_scaled, first_inverse_deviation, first_normalized, query_matrix_rows, key_matrix_rows, value_matrix_rows, attention_result, logged_total, second_centered_scaled, second_inverse_deviation, second_normalized, preactivation, activation_narrow = saved_tensors[layer_number]
            grad_low = running_gradient.astype(jnp.bfloat16)
            g_fc2 = jnp.dot(grad_low.T, activation_narrow, preferred_element_type=jnp.float32)
            g_bias_two = lax.optimization_barrier(jnp.sum(running_gradient, 0))
            d_pre = jnp.dot(grad_low, second_weight, preferred_element_type=jnp.float32) * gelu_slope(preactivation)
            d_pre_low = d_pre.astype(jnp.bfloat16)
            g_fc1 = jnp.dot(second_normalized.T, d_pre_low, preferred_element_type=jnp.float32)
            g_fc1_bias = lax.optimization_barrier(jnp.sum(d_pre, 0))
            second_normed_gradient = jnp.dot(d_pre_low, first_weight.T, preferred_element_type=jnp.float32)
            middle_gradient, second_gain_gradient, second_shift_gradient = layernorm_backward(second_normed_gradient, second_centered_scaled, second_inverse_deviation, vector_rows[5], running_gradient)
            mid_low = middle_gradient.astype(jnp.bfloat16)
            g_out = jnp.dot(mid_low.T, attention_result, preferred_element_type=jnp.float32)
            g_bias_out = lax.optimization_barrier(jnp.sum(middle_gradient, 0))
            d_att = jnp.dot(mid_low, backward_weight, preferred_element_type=jnp.float32).astype(jnp.bfloat16)
            d_query, d_key, d_value = attend_backward(split_heads(query_matrix_rows), split_heads(key_matrix_rows), split_heads(value_matrix_rows), split_heads(attention_result), split_heads(d_att), logged_total)
            d_query = d_query.reshape(SEQ, D)
            d_key = d_key.reshape(SEQ, D)
            d_value = d_value.reshape(SEQ, D)
            d_proj = jnp.stack([d_query, d_key, d_value], axis=1).astype(jnp.bfloat16).reshape(SEQ, 3 * D)
            g_qkv = jnp.dot(first_normalized.T, d_proj, preferred_element_type=jnp.float32).reshape(D, 3, D)
            first_normed_gradient = jnp.dot(d_proj, projection_weight.T, preferred_element_type=jnp.float32)
            running_gradient, first_gain_gradient, first_shift_gradient = layernorm_backward(first_normed_gradient, first_centered_scaled, first_inverse_deviation, vector_rows[0], middle_gradient)
            g_vec = jnp.stack([first_gain_gradient, first_shift_gradient, lax.optimization_barrier(jnp.sum(d_query, 0)), lax.optimization_barrier(jnp.sum(d_value, 0)), g_bias_out, second_gain_gradient, second_shift_gradient, g_bias_two])
            layer_grads[layer_number] = (g_qkv, g_out, g_fc1, g_fc2, g_vec, g_fc1_bias)
        stacked = tuple((jnp.stack([entry[which] for entry in layer_grads]) for which in range(6)))
        totals = tuple((total + part for total, part in zip(totals, stacked)))
        return (totals, (hidden_state * slot_live, running_gradient * slot_live))
    zero_totals = (jnp.zeros((LAYERS, D, 3, D), jnp.float32), jnp.zeros((LAYERS, D, D), jnp.float32), jnp.zeros((LAYERS, D, FF), jnp.float32), jnp.zeros((LAYERS, D, FF), jnp.float32), jnp.zeros((LAYERS, 8, D), jnp.float32), jnp.zeros((LAYERS, FF), jnp.float32))
    totals, (output, input_grad) = lax.scan(run_slot, zero_totals, (tokens, cotangent, live_all))
    params = (w_qkv, w_out, w_fc1, w_fc2, vec_small, fc1_bias)
    moments = (mom_qkv, mom_out, mom_fc1, mom_fc2, mom_vec, mom_bias)
    decays = (WEIGHT_DECAY, WEIGHT_DECAY, WEIGHT_DECAY, WEIGHT_DECAY, 0.0, 0.0)
    results = [adam_update(param, grad_total, moment, decay) for param, grad_total, moment, decay in zip(params, totals, moments, decays)]
    return (output, input_grad, totals[0], totals[1], totals[2], totals[3], totals[4], totals[5], results[0][0], results[1][0], results[2][0], results[3][0], results[4][0], results[5][0], results[0][1], results[1][1], results[2][1], results[3][1], results[4][1], results[5][1])
```

```python
import functools

import jax
import jax.numpy as jnp
from jax import lax
from jax.experimental import pallas as pl
from jax.experimental.pallas import tpu as pltpu
from jax.sharding import Mesh, PartitionSpec as P

HEAD = 64
STEP = 10
IMAGES = 4

NORM_EPS = 1e-06
ROOT_HALF = 0.7071067811865476
INV_ROOT_TWO_PI = 0.3989422804014327
LEARN_RATE = 0.01
BETA_ONE = 0.9
BETA_TWO = 0.999
ADAM_EPS = 1e-08
WEIGHT_DECAY = 0.05
CONTRACT_LAST = (((1,), (1,)), ((), ()))
CONTRACT_FIRST = (((0,), (0,)), ((), ()))
LOW = jnp.bfloat16
WIDE = jnp.float32
LANES = 128


def dot(left, right, dims=(((1,), (0,)), ((), ()))):
    return lax.dot_general(left, right, dims, preferred_element_type=WIDE)


def bits_of(axis):
    count = lax.axis_size(axis)
    return [1 << i for i in range(count.bit_length() - 1)]


def swap(value, axis, bit):
    count = lax.axis_size(axis)
    return lax.ppermute(value, axis, [(i, i ^ bit) for i in range(count)])


def bit_set(axis, bit):
    return (lax.axis_index(axis) // bit) % 2 == 1


def in_order(mine, arrived, axis, bit):
    upper = bit_set(axis, bit)
    return jnp.stack([jnp.where(upper, arrived, mine), jnp.where(upper, mine, arrived)])


def gather_step(mine, axis, bit):
    return in_order(mine, swap(mine, axis, bit), axis, bit)


def untangle(pieces, axis):
    for bit in bits_of(axis):
        upper = bit_set(axis, bit)
        pieces = [jnp.where(upper, pieces[d ^ bit], pieces[d]) for d in range(len(pieces))]
    return pieces


def line_in_order(value, axis):
    return untangle(
        [swap(value, axis, d) if d else value for d in range(lax.axis_size(axis))], axis
    )


MESH = pl.DeviceIdType.MESH


def greet(partners):
    barrier = pltpu.get_barrier_semaphore()
    for partner in partners:
        pl.semaphore_signal(barrier, inc=1, device_id=partner, device_id_type=MESH)
    pl.semaphore_wait(barrier, len(partners))


def partners_of(count):
    pos, img = lax.axis_index("pos"), lax.axis_index("img")
    bits = [1 << i for i in range(count.bit_length() - 1)]
    return [{"img": img ^ d} for d in range(1, IMAGES)] + [{"pos": pos ^ b} for b in bits]


def sends_of(count):
    bits = [1 << i for i in range(count.bit_length() - 1)]
    table = []
    for which, order in enumerate((bits, bits[::-1])):
        held = [0]
        for stage, bit in enumerate(order):
            table += [(which, stage, bit, d) for d in held]
            held = held + [d | bit for d in held]
    return table


def gather_kernel(count, pieces, *refs):
    blocks, wholes = refs[:pieces], refs[pieces : 2 * pieces]
    own_sem, near_send, near_recv, far_send, far_recv = refs[2 * pieces :]
    pos, img = lax.axis_index("pos"), lax.axis_index("img")
    rows = blocks[0].shape[0]
    table = sends_of(count)
    greet(partners_of(count))

    def place(p, q, first, blocks_wide):
        cols = blocks[p].shape[1]
        return wholes[p].at[
            pl.ds(pl.multiple_of(q * rows, rows), rows),
            pl.ds(pl.multiple_of(first * cols, cols), blocks_wide * cols),
        ]

    own, near, far = {}, {}, {}
    for p in range(pieces):
        own[p] = pltpu.make_async_copy(blocks[p], place(p, pos, img, 1), own_sem.at[p])
        own[p].start()
        for d in range(1, IMAGES):
            near[p, d] = pltpu.make_async_remote_copy(
                src_ref=blocks[p],
                dst_ref=place(p, pos, img, 1),
                send_sem=near_send.at[p, d],
                recv_sem=near_recv.at[p, d],
                device_id={"img": img ^ d},
                device_id_type=MESH,
            )
            near[p, d].start()

    def start(p, entries):
        for e in entries:
            which, stage, bit, offset = table[e]
            there = place(p, pos ^ offset, which * (IMAGES // 2), IMAGES // 2)
            far[p, e] = pltpu.make_async_remote_copy(
                src_ref=there,
                dst_ref=there,
                send_sem=far_send.at[p, e],
                recv_sem=far_recv.at[p, e],
                device_id={"pos": pos ^ bit},
                device_id_type=MESH,
            )
            far[p, e].start()

    def forward(p):
        for e, (which, stage, bit, offset) in enumerate(table):
            if offset:
                last = max(
                    (f for f, t in enumerate(table) if t[0] == which and offset & t[2]),
                    key=lambda f: table[f][1],
                )
                source = next(
                    f
                    for f, t in enumerate(table)
                    if t[0] == which and t[2] == table[last][2] and t[3] == offset ^ table[last][2]
                )
                if (p, source) not in landed:
                    far[p, source].wait_recv()
                    landed.add((p, source))
                start(p, [e])

    landed = set()
    for p in range(pieces):
        own[p].wait()
        for d in range(1, IMAGES):
            near[p, d].wait_recv()
        start(p, [e for e, t in enumerate(table) if t[3] == 0])
        if p:
            forward(p - 1)
    forward(pieces - 1)
    for p in range(pieces):
        for d in range(1, IMAGES):
            near[p, d].wait_send()
        for e in range(len(table)):
            if (p, e) not in landed:
                far[p, e].wait_recv()
            far[p, e].wait_send()


def gather_plain(block):
    whole = lax.all_gather(block, ("img", "pos"))
    rows, cols = block.shape
    whole = whole.reshape(IMAGES, -1, cols)
    return jnp.concatenate([whole[i] for i in range(IMAGES)], axis=1)


def scatter_plain(grad):
    count = lax.axis_size("pos")
    parts = jnp.stack(jnp.split(grad, IMAGES, axis=1))
    parts = parts.reshape(IMAGES * count, grad.shape[0] // count, -1)
    return lax.psum_scatter(parts, ("img", "pos")).astype(WIDE)


def gather_weights(blocks):
    if any(b.shape[1] % LANES for b in blocks):
        plain = [gather_plain(b) if b.shape[1] % LANES else None for b in blocks]
        rest = iter(gather_weights([b for b in blocks if not b.shape[1] % LANES]))
        return [next(rest) if p is None else p for p in plain]
    count, pieces = lax.axis_size("pos"), len(blocks)
    copies = len(sends_of(count))
    moved = sum(2 * count * IMAGES * b.size for b in blocks)
    anywhere = pl.BlockSpec(memory_space=pl.ANY)
    return pl.pallas_call(
        functools.partial(gather_kernel, count, pieces),
        in_specs=[anywhere] * pieces,
        out_specs=[anywhere] * pieces,
        out_shape=[
            jax.ShapeDtypeStruct((count * b.shape[0], IMAGES * b.shape[1]), LOW) for b in blocks
        ],
        scratch_shapes=[
            pltpu.SemaphoreType.DMA((pieces,)),
            pltpu.SemaphoreType.DMA((pieces, IMAGES)),
            pltpu.SemaphoreType.DMA((pieces, IMAGES)),
            pltpu.SemaphoreType.DMA((pieces, copies)),
            pltpu.SemaphoreType.DMA((pieces, copies)),
        ],
        compiler_params=pltpu.CompilerParams(collective_id=0, has_side_effects=True),
        cost_estimate=pl.CostEstimate(flops=0, bytes_accessed=8 * moved, transcendentals=0),
    )(*blocks)


def receipts_of(count):
    bits = [1 << i for i in range(count.bit_length() - 1)]
    table = []
    for which, order in enumerate((bits[::-1], bits)):
        kept = list(range(count))
        for stage, bit in enumerate(order):
            kept = [d for d in kept if not d & bit]
            table += [(which, stage, bit, d) for d in kept]
    return table


CHUNK = 32


def scatter_kernel(count, pieces, *refs):
    grads, outs = refs[:pieces], refs[pieces : 2 * pieces]
    arrived, sums, near = refs[2 * pieces : 3 * pieces], refs[3 * pieces : 4 * pieces], refs[4 * pieces : 5 * pieces]
    far_send, far_recv, near_send, near_recv = refs[5 * pieces :]
    pos, img = lax.axis_index("pos"), lax.axis_index("img")
    rows = outs[0].shape[0]
    table = receipts_of(count)
    stages = max(t[1] for t in table) + 1
    half = IMAGES // 2
    greet(partners_of(count))
    far, close = {}, {}

    partial = {}

    def whole_part(p, which, offset):
        cols = outs[p].shape[1]
        return grads[p].at[
            pl.ds(pl.multiple_of((pos ^ offset) * rows, rows), rows),
            pl.ds(which * half * cols, half * cols),
        ]

    def send(p, stage):
        for e, (which, at, bit, offset) in enumerate(table):
            if at == stage:
                far[p, e] = pltpu.make_async_remote_copy(
                    src_ref=partial[p, which, offset | bit]
                    if stage
                    else whole_part(p, which, offset | bit),
                    dst_ref=arrived[p].at[e],
                    send_sem=far_send.at[p, e],
                    recv_sem=far_recv.at[p, e],
                    device_id={"pos": pos ^ bit},
                    device_id_type=MESH,
                )
                far[p, e].start()

    def add(p, stage):
        for e, (which, at, bit, offset) in enumerate(table):
            if at != stage:
                continue
            far[p, e].wait_recv()
            cols = outs[p].shape[1]
            before = partial[p, which, offset] if stage else whole_part(p, which, offset)
            slot = arrived[p].at[e]

            def body(i, carry, before=before, slot=slot, which=which, p=p, cols=cols):
                step = pl.ds(pl.multiple_of(i * CHUNK, CHUNK), CHUNK)
                total = (before[step, :].astype(WIDE) + slot[step, :].astype(WIDE)).astype(LOW)
                if stage < stages - 1:
                    slot[step, :] = total
                else:
                    for j in range(half):
                        sums[p][which * half + j, step] = total[:, j * cols : (j + 1) * cols]
                return carry

            lax.fori_loop(0, rows // CHUNK, body, 0)
            partial[p, which, offset] = slot

    def send_near(p):
        for d in range(1, IMAGES):
            close[p, d] = pltpu.make_async_remote_copy(
                src_ref=sums[p].at[img ^ d],
                dst_ref=near[p].at[d - 1],
                send_sem=near_send.at[p, d],
                recv_sem=near_recv.at[p, d],
                device_id={"img": img ^ d},
                device_id_type=MESH,
            )
            close[p, d].start()

    def finish(p):
        for d in range(1, IMAGES):
            close[p, d].wait_recv()

        def body(i, carry):
            step = pl.ds(pl.multiple_of(i * CHUNK, CHUNK), CHUNK)
            total = sums[p][img, step].astype(WIDE)
            for d in range(1, IMAGES):
                total += near[p][d - 1, step].astype(WIDE)
            outs[p][step, :] = total
            return carry

        lax.fori_loop(0, rows // CHUNK, body, 0)

    for turn in range(pieces + stages + 1):
        if turn < pieces:
            send(turn, 0)
        for stage in range(stages):
            p = turn - 1 - stage
            if 0 <= p < pieces:
                add(p, stage)
                if stage < stages - 1:
                    send(p, stage + 1)
                else:
                    send_near(p)
        p = turn - 1 - stages
        if 0 <= p < pieces:
            finish(p)
    for p in range(pieces):
        for e in range(len(table)):
            far[p, e].wait_send()
        for d in range(1, IMAGES):
            close[p, d].wait_send()


def scatter_grads(grads):
    if any(g.shape[1] // IMAGES % LANES for g in grads):
        plain = [scatter_plain(g) if g.shape[1] // IMAGES % LANES else None for g in grads]
        rest = iter(scatter_grads([g for g in grads if not g.shape[1] // IMAGES % LANES]))
        return [next(rest) if p is None else p for p in plain]
    count, pieces = lax.axis_size("pos"), len(grads)
    copies = len(receipts_of(count))
    shapes = [(g.shape[0] // count, g.shape[1] // IMAGES) for g in grads]
    in_vmem = pl.BlockSpec(memory_space=pltpu.VMEM)
    moved = sum(2 * g.size for g in grads)
    return pl.pallas_call(
        functools.partial(scatter_kernel, count, pieces),
        in_specs=[in_vmem] * pieces,
        out_specs=[in_vmem] * pieces,
        out_shape=[jax.ShapeDtypeStruct(s, WIDE) for s in shapes],
        scratch_shapes=[pltpu.VMEM((copies, r, IMAGES // 2 * c), LOW) for r, c in shapes]
        + [pltpu.VMEM((IMAGES, r, c), LOW) for r, c in shapes]
        + [pltpu.VMEM((IMAGES - 1, r, c), LOW) for r, c in shapes]
        + [
            pltpu.SemaphoreType.DMA((pieces, copies)),
            pltpu.SemaphoreType.DMA((pieces, copies)),
            pltpu.SemaphoreType.DMA((pieces, IMAGES)),
            pltpu.SemaphoreType.DMA((pieces, IMAGES)),
        ],
        compiler_params=pltpu.CompilerParams(
            collective_id=1, has_side_effects=True, vmem_limit_bytes=48 << 20
        ),
        cost_estimate=pl.CostEstimate(flops=0, bytes_accessed=8 * moved, transcendentals=0),
    )(*grads)


def group_sum(partial):
    for axis in ("core", "sub"):
        for bit in bits_of(axis):
            partial = partial + swap(partial.astype(LOW), axis, bit).astype(WIDE)
    return partial


def chip_sum(value):
    for axis in ("img", "pos"):
        for bit in bits_of(axis):
            value = value + swap(value, axis, bit)
    return value


def send_column(value, distance):
    return lax.ppermute(value, ("core", "img"), distance)


def to_images(slots):
    core, img = lax.axis_index("core"), lax.axis_index("img")
    pieces = []
    for distance in range(IMAGES):
        payload = jnp.where((img ^ distance) % 2 == 1, slots[1], slots[0])
        if distance:
            pairs = [
                (c * IMAGES + (i ^ distance), c * IMAGES + i)
                for c in range(2)
                for i in range(IMAGES)
                if i // 2 == c
            ]
            payload = send_column(payload, pairs)
        pieces.append(payload)
    pieces = untangle(pieces, "img")
    for bit in bits_of("sub"):
        pieces = [
            jnp.concatenate(list(gather_step(p, "sub", bit)), axis=-1) for p in pieces
        ]
    mine = jnp.concatenate(pieces, axis=-1)
    return jnp.where(img // 2 == core, mine, swap(mine, "core", 1))


def from_images(image):
    core, img, sub = lax.axis_index("core"), lax.axis_index("img"), lax.axis_index("sub")
    seq, width = image.shape
    subs = lax.axis_size("sub")
    share = width // (IMAGES * subs)
    image = image.reshape(seq, IMAGES, subs, share)
    if subs > 1:
        image = lax.dynamic_index_in_dim(image, sub, 2, keepdims=True)
    blocks = [image[:, i, 0] for i in range(IMAGES)]
    blocks = untangle(blocks, "img")
    pieces = [blocks[0]]
    for distance in range(1, IMAGES):
        pairs = [
            (c * IMAGES + i, c * IMAGES + (i ^ distance))
            for c in range(2)
            for i in range(IMAGES)
            if i // 2 == c
        ]
        pieces.append(send_column(blocks[distance], pairs))
    pieces = untangle(pieces, "img")
    return jnp.stack([jnp.where(core == 1, pieces[2 + s], pieces[s]) for s in range(2)])


def gelu_parts(value):
    return 0.5 * (1.0 + lax.erf(value * ROOT_HALF))


def norm_forward(hidden):
    mean = jnp.mean(hidden, -1, keepdims=True)
    spread = jnp.mean(hidden * hidden, -1, keepdims=True) - mean * mean
    inv = lax.rsqrt(spread + NORM_EPS)
    return (hidden - mean) * inv, inv


def norm_backward(d_normed, normed, inv, gain, carried):
    d_hat = d_normed * gain
    plain = jnp.mean(d_hat, -1, keepdims=True)
    crossed = jnp.mean(d_hat * normed, -1, keepdims=True)
    grad = carried + inv * (d_hat - plain - normed * crossed)
    return grad, jnp.sum(d_normed * normed, 0), jnp.sum(d_normed, 0)


def softmax_rows(query, key, seq):
    scores = dot(query, key, CONTRACT_LAST) * HEAD ** (-0.5)
    column = lax.broadcasted_iota(jnp.int32, scores.shape, 1)
    scores = jnp.where(column < seq, scores, -1e30)
    raised = jnp.exp(scores - jnp.max(scores, -1, keepdims=True))
    return raised * (1.0 / jnp.sum(raised, -1, keepdims=True))


def split_three(value, group):
    cuts = [value[:, i : i + group] for i in range(0, value.shape[1], group)]
    if len(cuts) == 3:
        return cuts
    return [jnp.concatenate(cuts[k::3], axis=1) for k in range(3)]


def attend_kernel(seq, group, proj_ref, o_ref):
    query, key, value = split_three(proj_ref[...], group)
    lane_head = lax.broadcasted_iota(jnp.int32, query.shape, 1) // HEAD
    total = jnp.zeros(query.shape, WIDE)
    for head in range(query.shape[1] // HEAD):
        own = lane_head == head
        probs = softmax_rows(jnp.where(own, query, jnp.zeros_like(query)), key, seq)
        total = jnp.where(own, dot(probs.astype(LOW), value), total)
    o_ref[...] = total.astype(LOW)


def attend_back_kernel(seq, group, proj_ref, o_ref, do_ref, dproj_ref, sq_ref, sv_ref):
    query, key, value = split_three(proj_ref[...], group)
    out, d_out = o_ref[...].astype(WIDE), do_ref[...]
    lane_head = lax.broadcasted_iota(jnp.int32, query.shape, 1) // HEAD
    d_query = jnp.zeros(query.shape, WIDE)
    d_key = jnp.zeros(query.shape, WIDE)
    d_value = jnp.zeros(query.shape, WIDE)
    for head in range(query.shape[1] // HEAD):
        own = lane_head == head
        probs = softmax_rows(jnp.where(own, query, jnp.zeros_like(query)), key, seq)
        d_own = jnp.where(own, d_out, jnp.zeros_like(d_out))
        d_value = jnp.where(own, dot(probs.astype(LOW), d_out, CONTRACT_FIRST), d_value)
        d_probs = dot(d_own, value, CONTRACT_LAST)
        delta = jnp.sum(d_own.astype(WIDE) * out, -1, keepdims=True)
        d_scores = (probs * (d_probs - delta) * HEAD ** (-0.5)).astype(LOW)
        d_query = jnp.where(own, dot(d_scores, key), d_query)
        d_key = jnp.where(own, dot(d_scores, query, CONTRACT_FIRST), d_key)
    for which, part in enumerate((d_query, d_key, d_value)):
        for j in range(part.shape[1] // group):
            at = (3 * j + which) * group
            dproj_ref[:, at : at + group] = part[:, j * group : (j + 1) * group].astype(LOW)
    sq_ref[...] = jnp.broadcast_to(jnp.sum(d_query, 0, keepdims=True), sq_ref.shape)
    sv_ref[...] = jnp.broadcast_to(jnp.sum(d_value, 0, keepdims=True), sv_ref.shape)


def attend_forward(proj, seq):
    rows, width = proj.shape[0], proj.shape[1] // 3
    group = width // IMAGES
    lanes = max(LANES, group)
    steps = width // lanes

    return pl.pallas_call(
        functools.partial(attend_kernel, seq, group),
        grid=(steps,),
        in_specs=[pl.BlockSpec((rows, 3 * lanes), lambda i: (0, i))],
        out_specs=pl.BlockSpec((rows, lanes), lambda i: (0, i)),
        out_shape=jax.ShapeDtypeStruct((rows, width), LOW),
        compiler_params=pltpu.CompilerParams(vmem_limit_bytes=32 << 20),
        cost_estimate=pl.CostEstimate(
            flops=8 * rows * rows * width,
            bytes_accessed=8 * rows * width,
            transcendentals=rows * rows * width // HEAD,
        ),
    )(proj)


def attend_backward(proj, out, d_out, seq):
    rows, width = out.shape
    group = width // IMAGES
    lanes = max(LANES, group)
    steps = width // lanes

    sums = pl.BlockSpec((8, lanes), lambda i: (0, i))
    column = pl.BlockSpec((rows, lanes), lambda i: (0, i))
    triple = pl.BlockSpec((rows, 3 * lanes), lambda i: (0, i))
    low = jax.ShapeDtypeStruct((rows, 3 * width), LOW)
    wide = jax.ShapeDtypeStruct((8, width), WIDE)
    return pl.pallas_call(
        functools.partial(attend_back_kernel, seq, group),
        grid=(steps,),
        in_specs=[triple, column, column],
        out_specs=[triple, sums, sums],
        out_shape=[low, wide, wide],
        compiler_params=pltpu.CompilerParams(vmem_limit_bytes=32 << 20),
        cost_estimate=pl.CostEstimate(
            flops=20 * rows * rows * width,
            bytes_accessed=16 * rows * width,
            transcendentals=rows * rows * width // HEAD,
        ),
    )(proj, out, d_out)


def adam_update(param, gradient, moments, decay):
    first = BETA_ONE * moments[0] + (1.0 - BETA_ONE) * gradient
    second = BETA_TWO * moments[1] + (1.0 - BETA_TWO) * gradient * gradient
    fix_one = 1.0 - BETA_ONE**STEP
    fix_two = 1.0 - BETA_TWO**STEP
    update = first / fix_one / (jnp.sqrt(second / fix_two) + ADAM_EPS) + decay * param
    return (param - LEARN_RATE * update, jnp.stack([first, second]))


def on_device(
    tokens,
    cotangent,
    image_counts,
    w_qkv,
    w_out,
    w_fc1,
    w_fc2,
    vec_small,
    fc1_bias,
    mom_qkv,
    mom_out,
    mom_fc1,
    mom_fc2,
    mom_vec,
    mom_bias,
):
    core, img, sub = lax.axis_index("core"), lax.axis_index("img"), lax.axis_index("sub")
    subs = lax.axis_size("sub")
    layers, rows = w_qkv.shape[0], w_qkv.shape[1]
    seq, feat = tokens.shape[1], tokens.shape[2]
    width = feat * IMAGES * subs
    hidden = fc1_bias.shape[1]
    padded = -(-seq // 16) * 16
    slot_live = jnp.stack([jnp.ones((), WIDE), (image_counts[0] == 2).astype(WIDE)])[:, None, None]

    def pad(image):
        return jnp.pad(image, ((0, padded - seq), (0, 0)))

    def cut(weight):
        lead = weight.shape[:-1] + (2, weight.shape[-1] // 2)
        pair = weight.reshape(lead)
        return [pair[..., which, :].reshape(rows, -1) for which in range(2)]

    blocks = []
    for n in range(layers):
        cuts = [cut(w[n]) for w in (w_qkv, w_out, w_fc1, w_fc2)]
        widths = [c[0].shape[1] for c in cuts]
        pair = [jnp.concatenate([c[which] for c in cuts], axis=1).astype(LOW) for which in range(2)]
        kept = jnp.where(core == 1, pair[1], pair[0])
        sent = jnp.where(core == 1, pair[0], pair[1])
        both = in_order(kept, swap(sent, "core", 1), "core", 1).reshape(2 * rows, -1)
        ends = [sum(widths[: k + 1]) for k in range(4)]
        blocks.append([both[:, e - w : e] for e, w in zip(ends, widths)])

    state = pad(to_images(tokens)).astype(WIDE)

    vec_rows = vec_small.shape[0] * vec_small.shape[1]
    small = jnp.concatenate(
        [vec_small.reshape(vec_rows, feat), fc1_bias.reshape(-1, feat)], axis=0
    )
    for bit in bits_of("sub"):
        small = gather_step(small.reshape((-1, 1) + small.shape[-2:]), "sub", bit)
    small = small.reshape((subs,) + small.shape[-2:])
    small = jnp.stack(line_in_order(small, "img"))
    vec_near = small[:, :, :vec_rows].reshape(
        (IMAGES, subs, vec_small.shape[0], vec_small.shape[1], feat)
    ).transpose(2, 3, 0, 1, 4)
    bias_near = small[:, :, vec_rows:].reshape(IMAGES, subs, layers, hidden).transpose(2, 0, 1, 3)

    def own_half(blocks_of):
        n = blocks_of.shape[-1] // 2
        lead = blocks_of.shape[:-3]
        cut = blocks_of.reshape(lead + (IMAGES, subs, 2, n))
        cut = lax.dynamic_index_in_dim(cut, sub, len(lead) + 1, keepdims=False)
        cut = lax.dynamic_index_in_dim(cut, core, len(lead) + 1, keepdims=False)
        return cut.reshape(lead + (IMAGES * n,))

    vec_half = own_half(vec_near)
    bias_half = own_half(bias_near)
    vec_full = vec_near.reshape(vec_small.shape[:2] + (width,))

    inner = IMAGES * feat // 2
    weights = [gather_weights(cut) for cut in blocks]

    saved = []
    for n in range(layers):
        qkv_weight, out_weight, first_weight, second_weight = weights[n]
        full = vec_full[n]
        hat_one, inv_one = norm_forward(state)
        normed_one = (hat_one * full[0] + full[1]).astype(LOW)
        shift = jnp.stack([vec_half[n, 2], jnp.zeros_like(vec_half[n, 2]), vec_half[n, 3]])
        shift = shift.reshape(3, IMAGES, -1).transpose(1, 0, 2).reshape(-1)
        proj = (dot(normed_one, qkv_weight) + shift).astype(LOW)
        attended = attend_forward(proj, seq)
        middle = state + group_sum(dot(attended, out_weight, CONTRACT_LAST)) + full[4]
        hat_two, inv_two = norm_forward(middle)
        normed_two = (hat_two * full[5] + full[6]).astype(LOW)
        before = dot(normed_two, first_weight) + bias_half[n]
        active = (before * gelu_parts(before)).astype(LOW)
        branch = dot(active, second_weight, CONTRACT_LAST)
        saved.append(
            (hat_one, inv_one, normed_one, proj, attended, hat_two, inv_two, normed_two, before, active)
        )
        state = middle + group_sum(branch) + full[7]
    output = from_images(state[:seq].astype(LOW)).astype(WIDE) * slot_live

    gradient = (cotangent * slot_live).astype(LOW)
    gradient = pad(to_images(gradient)).astype(WIDE)
    big = [None] * layers
    small_grads = [None] * layers
    for n in reversed(range(layers)):
        qkv_weight, out_weight, first_weight, second_weight = weights[n]
        full = vec_full[n]
        (hat_one, inv_one, normed_one, proj, attended, hat_two, inv_two, normed_two, before, active) = saved[n]
        grad_low = gradient.astype(LOW)
        g_second = dot(grad_low, active, CONTRACT_FIRST).astype(LOW)
        g_last = jnp.sum(gradient, 0)
        slope = gelu_parts(before) + before * jnp.exp(-0.5 * before * before) * INV_ROOT_TWO_PI
        d_before = dot(grad_low, second_weight) * slope
        d_low = d_before.astype(LOW)
        g_bias = jnp.sum(d_before, 0)
        g_first = dot(normed_two, d_low, CONTRACT_FIRST).astype(LOW)
        d_normed = group_sum(dot(d_low, first_weight, CONTRACT_LAST))
        middle_grad, g_gain_two, g_shift_two = norm_backward(
            d_normed, hat_two, inv_two, full[5], gradient
        )
        mid_low = middle_grad.astype(LOW)
        g_out_bias = jnp.sum(middle_grad, 0)
        g_out = dot(mid_low, attended, CONTRACT_FIRST).astype(LOW)
        d_attended = dot(mid_low, out_weight).astype(LOW)
        d_proj, sum_query, sum_value = attend_backward(proj, attended, d_attended, seq)
        g_qkv = dot(normed_one, d_proj, CONTRACT_FIRST).astype(LOW)
        d_normed = group_sum(dot(d_proj, qkv_weight, CONTRACT_LAST))
        gradient, g_gain_one, g_shift_one = norm_backward(
            d_normed, hat_one, inv_one, full[0], middle_grad
        )
        big[n] = scatter_grads([g_second, g_first, g_out, g_qkv])[::-1]
        of_features = jnp.stack(
            [g_gain_one, g_shift_one, g_out_bias, g_gain_two, g_shift_two, g_last]
        )
        small_grads[n] = chip_sum(
            jnp.concatenate(
                [of_features.reshape(-1), sum_query[0], sum_value[0], g_bias]
            ).reshape(-1, LANES)
        ).reshape(-1)
    input_grad = from_images(gradient[:seq].astype(LOW)).astype(WIDE) * slot_live

    def both_halves(block):
        block = block.reshape(2, rows, -1)
        kept = jnp.where(core == 1, block[1], block[0])
        sent = jnp.where(core == 1, block[0], block[1]).astype(LOW)
        return in_order(kept, swap(sent, "core", 1).astype(WIDE), "core", 1)

    grads = [[], [], [], []]
    for n in range(layers):
        s_qkv, s_out, s_first, s_second = [both_halves(b) for b in big[n]]
        s_qkv = s_qkv.reshape(2, rows, 3, feat // 2).transpose(1, 2, 0, 3)
        grads[0].append(s_qkv.reshape(rows, 3, feat))
        grads[1].append(s_out.transpose(1, 0, 2).reshape(rows, feat))
        grads[2].append(s_first.transpose(1, 0, 2).reshape(rows, hidden))
        grads[3].append(s_second.transpose(1, 0, 2).reshape(rows, hidden))

    vec_rows_of = []
    bias_rows_of = []
    for n in range(layers):
        total = small_grads[n]
        whole = total[: 6 * width].reshape(6, IMAGES, subs, feat)
        whole = lax.dynamic_index_in_dim(whole, img, 1, keepdims=False)
        whole = lax.dynamic_index_in_dim(whole, sub, 1, keepdims=False)
        split = total[6 * width : 6 * width + 2 * inner].reshape(2, IMAGES, feat // 2)
        split = lax.dynamic_index_in_dim(split, img, 1, keepdims=False)
        fc = total[6 * width + 2 * inner :].reshape(IMAGES, hidden // 2)
        fc = lax.dynamic_index_in_dim(fc, img, 0, keepdims=False)
        mine = jnp.concatenate([split.reshape(-1), fc])
        pair = gather_step(mine.reshape(-1, LANES // 2), "core", 1).reshape(2, -1)
        split = pair[:, :feat].reshape(2, 2, feat // 2).transpose(1, 0, 2).reshape(2, feat)
        vec_rows_of.append(
            jnp.stack(
                [whole[0], whole[1], split[0], split[1], whole[2], whole[3], whole[4], whole[5]]
            )
        )
        bias_rows_of.append(pair[:, feat:].reshape(-1))

    totals = tuple(jnp.stack(g) for g in grads) + (jnp.stack(vec_rows_of), jnp.stack(bias_rows_of))
    params = (w_qkv, w_out, w_fc1, w_fc2, vec_small, fc1_bias)
    moments = (mom_qkv, mom_out, mom_fc1, mom_fc2, mom_vec, mom_bias)
    decays = (WEIGHT_DECAY, WEIGHT_DECAY, WEIGHT_DECAY, WEIGHT_DECAY, 0.0, 0.0)
    results = [
        adam_update(param, total, moment, decay)
        for param, total, moment, decay in zip(params, totals, moments, decays)
    ]
    return (
        (output, input_grad)
        + totals
        + tuple(r[0] for r in results)
        + tuple(r[1] for r in results)
    )


def solution(mesh):
    dp, tensor = mesh.shape["dp"], mesh.shape["tensor"]
    inner = Mesh(
        mesh.devices.reshape(dp // 2, 2, IMAGES, tensor // IMAGES), ("pos", "core", "img", "sub")
    )
    rows, cols = ("pos", "core"), ("img", "sub")
    images = P(rows, None, cols)
    weight = [P(None, rows, None, cols)] + [P(None, rows, cols)] * 3
    moment = [P(None, None, rows, None, cols)] + [P(None, None, rows, cols)] * 3
    vector = [P(None, None, cols), P(None, cols)]
    moment_vector = [P(None, None, None, cols), P(None, None, cols)]
    return jax.shard_map(
        on_device,
        mesh=inner,
        in_specs=tuple([images, images, P(rows)] + weight + vector + moment + moment_vector),
        out_specs=tuple(
            [images, images] + weight + vector + weight + vector + moment + moment_vector
        ),
        check_vma=False,
    )
```

```python
import functools

import jax
import jax.numpy as jnp
from jax import lax
from jax.experimental import pallas as pl
from jax.experimental.pallas import tpu as pltpu
from jax.sharding import Mesh, PartitionSpec as P

HEAD = 64
STEP = 10
IMAGES = 4

NORM_EPS = 1e-06
ROOT_HALF = 0.7071067811865476
INV_ROOT_TWO_PI = 0.3989422804014327
LEARN_RATE = 0.01
BETA_ONE = 0.9
BETA_TWO = 0.999
ADAM_EPS = 1e-08
WEIGHT_DECAY = 0.05
CONTRACT_LAST = (((1,), (1,)), ((), ()))
CONTRACT_FIRST = (((0,), (0,)), ((), ()))
LOW = jnp.bfloat16
WIDE = jnp.float32
LANES = 128


def dot(left, right, dims=(((1,), (0,)), ((), ()))):
    return lax.dot_general(left, right, dims, preferred_element_type=WIDE)


def bits_of(axis):
    count = lax.axis_size(axis)
    return [1 << i for i in range(count.bit_length() - 1)]


def swap(value, axis, bit):
    count = lax.axis_size(axis)
    return lax.ppermute(value, axis, [(i, i ^ bit) for i in range(count)])


def bit_set(axis, bit):
    return (lax.axis_index(axis) // bit) % 2 == 1


def in_order(mine, arrived, axis, bit):
    upper = bit_set(axis, bit)
    return jnp.stack([jnp.where(upper, arrived, mine), jnp.where(upper, mine, arrived)])


def gather_step(mine, axis, bit):
    return in_order(mine, swap(mine, axis, bit), axis, bit)


def untangle(pieces, axis):
    for bit in bits_of(axis):
        upper = bit_set(axis, bit)
        pieces = [jnp.where(upper, pieces[d ^ bit], pieces[d]) for d in range(len(pieces))]
    return pieces


def line_in_order(value, axis):
    return untangle(
        [swap(value, axis, d) if d else value for d in range(lax.axis_size(axis))], axis
    )


MESH = pl.DeviceIdType.MESH


def greet(partners):
    barrier = pltpu.get_barrier_semaphore()
    for partner in partners:
        pl.semaphore_signal(barrier, inc=1, device_id=partner, device_id_type=MESH)
    pl.semaphore_wait(barrier, len(partners))


def partners_of(count):
    pos, img = lax.axis_index("pos"), lax.axis_index("img")
    bits = [1 << i for i in range(count.bit_length() - 1)]
    twin = [{"core": 1 - lax.axis_index("core")}]
    return twin + [{"img": img ^ d} for d in range(1, IMAGES)] + [{"pos": pos ^ b} for b in bits]


def sends_of(count):
    bits = [1 << i for i in range(count.bit_length() - 1)]
    table = []
    for which, order in enumerate((bits, bits[::-1])):
        held = [0]
        for stage, bit in enumerate(order):
            table += [(which, stage, bit, d) for d in held]
            held = held + [d | bit for d in held]
    return table


def gather_kernel(count, kinds, *refs):
    pieces = len(kinds)
    shards, wholes = refs[:pieces], refs[pieces : 2 * pieces]
    own_sem, twin_send, twin_recv, near_send, near_recv, far_send, far_recv = refs[2 * pieces :]
    pos, img, core = lax.axis_index("pos"), lax.axis_index("img"), lax.axis_index("core")
    half_rows = shards[0].shape[0]
    rows = 2 * half_rows
    table = sends_of(count)
    greet(partners_of(count))

    def place(p, q, first, blocks_wide):
        cols = shards[p].shape[1] // 2
        return wholes[p].at[
            pl.ds(pl.multiple_of(q * rows, rows), rows),
            pl.ds(pl.multiple_of(first * cols, cols), blocks_wide * cols),
        ]

    own, twin, near, far = {}, {}, {}, {}
    for p in range(pieces):
        share = shards[p].shape[1] // (2 * kinds[p])
        for k in range(kinds[p]):
            first = (img * kinds[p] + k) * share
            there = wholes[p].at[
                pl.ds(pl.multiple_of(pos * rows + core * half_rows, half_rows), half_rows),
                pl.ds(pl.multiple_of(first, share), share),
            ]

            def columns(which, p=p, k=k, share=share):
                return shards[p].at[:, pl.ds(pl.multiple_of((2 * k + which) * share, share), share)]

            twin[p, k] = pltpu.make_async_remote_copy(
                src_ref=columns(1 - core),
                dst_ref=there,
                send_sem=twin_send.at[p, k],
                recv_sem=twin_recv.at[p, k],
                device_id={"core": 1 - core},
                device_id_type=MESH,
            )
            twin[p, k].start()
            own[p, k] = pltpu.make_async_copy(columns(core), there, own_sem.at[p, k])
            own[p, k].start()

    def start_near(p):
        for k in range(kinds[p]):
            own[p, k].wait()
            twin[p, k].wait_recv()
        for d in range(1, IMAGES):
            near[p, d] = pltpu.make_async_remote_copy(
                src_ref=place(p, pos, img, 1),
                dst_ref=place(p, pos, img, 1),
                send_sem=near_send.at[p, d],
                recv_sem=near_recv.at[p, d],
                device_id={"img": img ^ d},
                device_id_type=MESH,
            )
            near[p, d].start()

    def start(p, entries):
        for e in entries:
            which, stage, bit, offset = table[e]
            there = place(p, pos ^ offset, which * (IMAGES // 2), IMAGES // 2)
            far[p, e] = pltpu.make_async_remote_copy(
                src_ref=there,
                dst_ref=there,
                send_sem=far_send.at[p, e],
                recv_sem=far_recv.at[p, e],
                device_id={"pos": pos ^ bit},
                device_id_type=MESH,
            )
            far[p, e].start()

    def forward(p):
        for e, (which, stage, bit, offset) in enumerate(table):
            if offset:
                last = max(
                    (f for f, t in enumerate(table) if t[0] == which and offset & t[2]),
                    key=lambda f: table[f][1],
                )
                source = next(
                    f
                    for f, t in enumerate(table)
                    if t[0] == which and t[2] == table[last][2] and t[3] == offset ^ table[last][2]
                )
                if (p, source) not in landed:
                    far[p, source].wait_recv()
                    landed.add((p, source))
                start(p, [e])

    landed = set()
    for p in range(min(AHEAD, pieces)):
        start_near(p)
    for p in range(pieces):
        if p + AHEAD < pieces:
            start_near(p + AHEAD)
        for d in range(1, IMAGES):
            near[p, d].wait_recv()
        start(p, [e for e, t in enumerate(table) if t[3] == 0])
        if p:
            forward(p - 1)
    forward(pieces - 1)
    for p in range(pieces):
        for k in range(kinds[p]):
            twin[p, k].wait_send()
        for d in range(1, IMAGES):
            near[p, d].wait_send()
        for e in range(len(table)):
            if (p, e) not in landed:
                far[p, e].wait_recv()
            far[p, e].wait_send()


def cut_halves(shard, kinds):
    pair = shard.reshape(shard.shape[0], kinds, 2, -1)
    return [pair[:, :, which].reshape(shard.shape[0], -1) for which in range(2)]


def gather_plain(shard, kinds):
    core = lax.axis_index("core")
    pair = cut_halves(shard, kinds)
    kept = jnp.where(core == 1, pair[1], pair[0])
    sent = jnp.where(core == 1, pair[0], pair[1])
    block = in_order(kept, swap(sent, "core", 1), "core", 1).reshape(2 * shard.shape[0], -1)
    whole = lax.all_gather(block, ("img", "pos")).reshape(IMAGES, -1, block.shape[1])
    return jnp.concatenate([whole[i] for i in range(IMAGES)], axis=1)


def scatter_plain(grad, kinds):
    core, count = lax.axis_index("core"), lax.axis_size("pos")
    parts = jnp.stack(jnp.split(grad, IMAGES, axis=1))
    parts = parts.reshape(IMAGES * count, grad.shape[0] // count, -1)
    block = lax.psum_scatter(parts, ("img", "pos")).astype(WIDE)
    block = block.reshape(2, block.shape[0] // 2, -1)
    kept = jnp.where(core == 1, block[1], block[0])
    sent = jnp.where(core == 1, block[0], block[1]).astype(LOW)
    both = in_order(kept, swap(sent, "core", 1).astype(WIDE), "core", 1)
    both = both.reshape(2, both.shape[1], kinds, -1).transpose(1, 2, 0, 3)
    return both.reshape(both.shape[0], -1)


def aligned(width, kinds):
    return width // (2 * kinds) % LANES == 0


def gather_weights(shards, kinds):
    if not all(aligned(w.shape[1], k) for w, k in zip(shards, kinds)):
        good = [i for i, w in enumerate(shards) if aligned(w.shape[1], kinds[i])]
        done = dict(zip(good, gather_weights([shards[i] for i in good], [kinds[i] for i in good])))
        return [
            done[i] if i in done else gather_plain(w, kinds[i]) for i, w in enumerate(shards)
        ]
    count, pieces = lax.axis_size("pos"), len(shards)
    copies, most = len(sends_of(count)), max(kinds)
    moved = sum(2 * count * IMAGES * w.size for w in shards)
    anywhere = pl.BlockSpec(memory_space=pl.ANY)
    return pl.pallas_call(
        functools.partial(gather_kernel, count, tuple(kinds)),
        in_specs=[anywhere] * pieces,
        out_specs=[anywhere] * pieces,
        out_shape=[
            jax.ShapeDtypeStruct((count * 2 * w.shape[0], IMAGES * w.shape[1] // 2), LOW)
            for w in shards
        ],
        scratch_shapes=[
            pltpu.SemaphoreType.DMA((pieces, most)),
            pltpu.SemaphoreType.DMA((pieces, most)),
            pltpu.SemaphoreType.DMA((pieces, most)),
            pltpu.SemaphoreType.DMA((pieces, IMAGES)),
            pltpu.SemaphoreType.DMA((pieces, IMAGES)),
            pltpu.SemaphoreType.DMA((pieces, copies)),
            pltpu.SemaphoreType.DMA((pieces, copies)),
        ],
        compiler_params=pltpu.CompilerParams(collective_id=0, has_side_effects=True),
        cost_estimate=pl.CostEstimate(flops=0, bytes_accessed=8 * moved, transcendentals=0),
    )(*shards)


def receipts_of(count):
    bits = [1 << i for i in range(count.bit_length() - 1)]
    table = []
    for which, order in enumerate((bits[::-1], bits)):
        kept = list(range(count))
        for stage, bit in enumerate(order):
            kept = [d for d in kept if not d & bit]
            table += [(which, stage, bit, d) for d in kept]
    return table


CHUNK = 32
AHEAD = 1


def scatter_kernel(count, kinds, *refs):
    pieces = len(kinds)
    grads, outs, arrived, sums, near, gone, come = [
        refs[i * pieces : (i + 1) * pieces] for i in range(7)
    ]
    far_send, far_recv, near_send, near_recv, twin_send, twin_recv = refs[7 * pieces :]
    pos, img, core = lax.axis_index("pos"), lax.axis_index("img"), lax.axis_index("core")
    half_rows = outs[0].shape[0]
    rows = 2 * half_rows
    table = receipts_of(count)
    stages = max(t[1] for t in table) + 1
    half = IMAGES // 2
    greet(partners_of(count))
    far, close, twin = {}, {}, {}

    partial = {}

    def whole_part(p, which, offset):
        cols = outs[p].shape[1] // 2
        return grads[p].at[
            pl.ds(pl.multiple_of((pos ^ offset) * rows, rows), rows),
            pl.ds(which * half * cols, half * cols),
        ]

    def send(p, stage):
        for e, (which, at, bit, offset) in enumerate(table):
            if at == stage:
                far[p, e] = pltpu.make_async_remote_copy(
                    src_ref=partial[p, which, offset | bit]
                    if stage
                    else whole_part(p, which, offset | bit),
                    dst_ref=arrived[p].at[e],
                    send_sem=far_send.at[p, e],
                    recv_sem=far_recv.at[p, e],
                    device_id={"pos": pos ^ bit},
                    device_id_type=MESH,
                )
                far[p, e].start()

    def add(p, stage):
        for e, (which, at, bit, offset) in enumerate(table):
            if at != stage:
                continue
            far[p, e].wait_recv()
            cols = outs[p].shape[1] // 2
            before = partial[p, which, offset] if stage else whole_part(p, which, offset)
            slot = arrived[p].at[e]

            def body(i, carry, before=before, slot=slot, which=which, p=p, cols=cols):
                step = pl.ds(pl.multiple_of(i * CHUNK, CHUNK), CHUNK)
                total = (before[step, :].astype(WIDE) + slot[step, :].astype(WIDE)).astype(LOW)
                if stage < stages - 1:
                    slot[step, :] = total
                else:
                    for j in range(half):
                        sums[p][which * half + j, step] = total[:, j * cols : (j + 1) * cols]
                return carry

            lax.fori_loop(0, rows // CHUNK, body, 0)
            partial[p, which, offset] = slot

    def send_near(p):
        for d in range(1, IMAGES):
            close[p, d] = pltpu.make_async_remote_copy(
                src_ref=sums[p].at[img ^ d],
                dst_ref=near[p].at[d - 1],
                send_sem=near_send.at[p, d],
                recv_sem=near_recv.at[p, d],
                device_id={"img": img ^ d},
                device_id_type=MESH,
            )
            close[p, d].start()

    def columns(p, k, which):
        share = outs[p].shape[1] // (2 * kinds[p])
        return pl.ds(pl.multiple_of((2 * k + which) * share, share), share)

    def finish(p):
        share = outs[p].shape[1] // (2 * kinds[p])
        for d in range(1, IMAGES):
            close[p, d].wait_recv()

        def total_of(first):
            step = pl.ds(pl.multiple_of(first, CHUNK), CHUNK)
            total = sums[p][img, step].astype(WIDE)
            for d in range(1, IMAGES):
                total += near[p][d - 1, step].astype(WIDE)
            return total

        def other(i, carry):
            step = pl.ds(pl.multiple_of(i * CHUNK, CHUNK), CHUNK)
            gone[p][step, :] = total_of((1 - core) * half_rows + i * CHUNK).astype(LOW)
            return carry

        lax.fori_loop(0, half_rows // CHUNK, other, 0)
        twin[p] = pltpu.make_async_remote_copy(
            src_ref=gone[p],
            dst_ref=come[p],
            send_sem=twin_send.at[p],
            recv_sem=twin_recv.at[p],
            device_id={"core": 1 - core},
            device_id_type=MESH,
        )
        twin[p].start()

        def mine(i, carry):
            step = pl.ds(pl.multiple_of(i * CHUNK, CHUNK), CHUNK)
            total = total_of(core * half_rows + i * CHUNK)
            for k in range(kinds[p]):
                outs[p][step, columns(p, k, core)] = total[:, k * share : (k + 1) * share]
            return carry

        lax.fori_loop(0, half_rows // CHUNK, mine, 0)

    def close_twin(p):
        share = outs[p].shape[1] // (2 * kinds[p])
        twin[p].wait_recv()

        def body(i, carry):
            step = pl.ds(pl.multiple_of(i * CHUNK, CHUNK), CHUNK)
            total = come[p][step, :].astype(WIDE)
            for k in range(kinds[p]):
                outs[p][step, columns(p, k, 1 - core)] = total[:, k * share : (k + 1) * share]
            return carry

        lax.fori_loop(0, half_rows // CHUNK, body, 0)

    for turn in range(pieces + stages + 2):
        if turn < pieces:
            send(turn, 0)
        for stage in range(stages):
            p = turn - 1 - stage
            if 0 <= p < pieces:
                add(p, stage)
                if stage < stages - 1:
                    send(p, stage + 1)
                else:
                    send_near(p)
        p = turn - 1 - stages
        if 0 <= p < pieces:
            finish(p)
        p -= 1
        if 0 <= p < pieces:
            close_twin(p)
    for p in range(pieces):
        twin[p].wait_send()
        for e in range(len(table)):
            far[p, e].wait_send()
        for d in range(1, IMAGES):
            close[p, d].wait_send()


def scatter_grads(grads, kinds):
    widths = [2 * g.shape[1] // IMAGES for g in grads]
    if not all(aligned(w, k) for w, k in zip(widths, kinds)):
        good = [i for i, w in enumerate(widths) if aligned(w, kinds[i])]
        done = dict(zip(good, scatter_grads([grads[i] for i in good], [kinds[i] for i in good])))
        return [
            done[i] if i in done else scatter_plain(g, kinds[i]) for i, g in enumerate(grads)
        ]
    count, pieces = lax.axis_size("pos"), len(grads)
    copies = len(receipts_of(count))
    shapes = [(g.shape[0] // count, g.shape[1] // IMAGES) for g in grads]
    in_vmem = pl.BlockSpec(memory_space=pltpu.VMEM)
    moved = sum(2 * g.size for g in grads)
    return pl.pallas_call(
        functools.partial(scatter_kernel, count, tuple(kinds)),
        in_specs=[in_vmem] * pieces,
        out_specs=[in_vmem] * pieces,
        out_shape=[jax.ShapeDtypeStruct((r // 2, 2 * c), WIDE) for r, c in shapes],
        scratch_shapes=[pltpu.VMEM((copies, r, IMAGES // 2 * c), LOW) for r, c in shapes]
        + [pltpu.VMEM((IMAGES, r, c), LOW) for r, c in shapes]
        + [pltpu.VMEM((IMAGES - 1, r, c), LOW) for r, c in shapes]
        + [pltpu.VMEM((r // 2, c), LOW) for r, c in shapes]
        + [pltpu.VMEM((r // 2, c), LOW) for r, c in shapes]
        + [
            pltpu.SemaphoreType.DMA((pieces, copies)),
            pltpu.SemaphoreType.DMA((pieces, copies)),
            pltpu.SemaphoreType.DMA((pieces, IMAGES)),
            pltpu.SemaphoreType.DMA((pieces, IMAGES)),
            pltpu.SemaphoreType.DMA((pieces,)),
            pltpu.SemaphoreType.DMA((pieces,)),
        ],
        compiler_params=pltpu.CompilerParams(
            collective_id=1, has_side_effects=True, vmem_limit_bytes=48 << 20
        ),
        cost_estimate=pl.CostEstimate(flops=0, bytes_accessed=8 * moved, transcendentals=0),
    )(*grads)


def group_sum(partial):
    for axis in ("core", "sub"):
        for bit in bits_of(axis):
            partial = partial + swap(partial.astype(LOW), axis, bit).astype(WIDE)
    return partial


def chip_sum(value):
    for axis in ("img", "pos"):
        for bit in bits_of(axis):
            value = value + swap(value, axis, bit)
    return value


def send_column(value, distance):
    return lax.ppermute(value, ("core", "img"), distance)


def to_images(slots):
    core, img = lax.axis_index("core"), lax.axis_index("img")
    pieces = []
    for distance in range(IMAGES):
        payload = jnp.where((img ^ distance) % 2 == 1, slots[1], slots[0])
        if distance:
            pairs = [
                (c * IMAGES + (i ^ distance), c * IMAGES + i)
                for c in range(2)
                for i in range(IMAGES)
                if i // 2 == c
            ]
            payload = send_column(payload, pairs)
        pieces.append(payload)
    pieces = untangle(pieces, "img")
    for bit in bits_of("sub"):
        pieces = [
            jnp.concatenate(list(gather_step(p, "sub", bit)), axis=-1) for p in pieces
        ]
    mine = jnp.concatenate(pieces, axis=-1)
    return jnp.where(img // 2 == core, mine, swap(mine, "core", 1))


def from_images(image):
    core, img, sub = lax.axis_index("core"), lax.axis_index("img"), lax.axis_index("sub")
    seq, width = image.shape
    subs = lax.axis_size("sub")
    share = width // (IMAGES * subs)
    image = image.reshape(seq, IMAGES, subs, share)
    if subs > 1:
        image = lax.dynamic_index_in_dim(image, sub, 2, keepdims=True)
    blocks = [image[:, i, 0] for i in range(IMAGES)]
    blocks = untangle(blocks, "img")
    pieces = [blocks[0]]
    for distance in range(1, IMAGES):
        pairs = [
            (c * IMAGES + i, c * IMAGES + (i ^ distance))
            for c in range(2)
            for i in range(IMAGES)
            if i // 2 == c
        ]
        pieces.append(send_column(blocks[distance], pairs))
    pieces = untangle(pieces, "img")
    return jnp.stack([jnp.where(core == 1, pieces[2 + s], pieces[s]) for s in range(2)])


def gelu_parts(value):
    return 0.5 * (1.0 + lax.erf(value * ROOT_HALF))


def norm_forward(hidden):
    mean = jnp.mean(hidden, -1, keepdims=True)
    spread = jnp.mean(hidden * hidden, -1, keepdims=True) - mean * mean
    inv = lax.rsqrt(spread + NORM_EPS)
    return (hidden - mean) * inv, inv


def norm_backward(d_normed, normed, inv, gain, carried):
    d_hat = d_normed * gain
    plain = jnp.mean(d_hat, -1, keepdims=True)
    crossed = jnp.mean(d_hat * normed, -1, keepdims=True)
    grad = carried + inv * (d_hat - plain - normed * crossed)
    return grad, jnp.sum(d_normed * normed, 0), jnp.sum(d_normed, 0)


def softmax_rows(query, key, seq):
    scores = dot(query, key, CONTRACT_LAST) * HEAD ** (-0.5)
    column = lax.broadcasted_iota(jnp.int32, scores.shape, 1)
    scores = jnp.where(column < seq, scores, -1e30)
    raised = jnp.exp(scores - jnp.max(scores, -1, keepdims=True))
    return raised * (1.0 / jnp.sum(raised, -1, keepdims=True))


def split_three(value, group):
    cuts = [value[:, i : i + group] for i in range(0, value.shape[1], group)]
    if len(cuts) == 3:
        return cuts
    return [jnp.concatenate(cuts[k::3], axis=1) for k in range(3)]


def attend_kernel(seq, group, proj_ref, o_ref):
    query, key, value = split_three(proj_ref[...], group)
    lane_head = lax.broadcasted_iota(jnp.int32, query.shape, 1) // HEAD
    total = jnp.zeros(query.shape, WIDE)
    for head in range(query.shape[1] // HEAD):
        own = lane_head == head
        probs = softmax_rows(jnp.where(own, query, jnp.zeros_like(query)), key, seq)
        total = jnp.where(own, dot(probs.astype(LOW), value), total)
    o_ref[...] = total.astype(LOW)


def attend_back_kernel(seq, group, proj_ref, o_ref, do_ref, dproj_ref, sq_ref, sv_ref):
    query, key, value = split_three(proj_ref[...], group)
    out, d_out = o_ref[...].astype(WIDE), do_ref[...]
    lane_head = lax.broadcasted_iota(jnp.int32, query.shape, 1) // HEAD
    d_query = jnp.zeros(query.shape, WIDE)
    d_key = jnp.zeros(query.shape, WIDE)
    d_value = jnp.zeros(query.shape, WIDE)
    for head in range(query.shape[1] // HEAD):
        own = lane_head == head
        probs = softmax_rows(jnp.where(own, query, jnp.zeros_like(query)), key, seq)
        d_own = jnp.where(own, d_out, jnp.zeros_like(d_out))
        d_value = jnp.where(own, dot(probs.astype(LOW), d_out, CONTRACT_FIRST), d_value)
        d_probs = dot(d_own, value, CONTRACT_LAST)
        delta = jnp.sum(d_own.astype(WIDE) * out, -1, keepdims=True)
        d_scores = (probs * (d_probs - delta) * HEAD ** (-0.5)).astype(LOW)
        d_query = jnp.where(own, dot(d_scores, key), d_query)
        d_key = jnp.where(own, dot(d_scores, query, CONTRACT_FIRST), d_key)
    for which, part in enumerate((d_query, d_key, d_value)):
        for j in range(part.shape[1] // group):
            at = (3 * j + which) * group
            dproj_ref[:, at : at + group] = part[:, j * group : (j + 1) * group].astype(LOW)
    sq_ref[...] = jnp.broadcast_to(jnp.sum(d_query, 0, keepdims=True), sq_ref.shape)
    sv_ref[...] = jnp.broadcast_to(jnp.sum(d_value, 0, keepdims=True), sv_ref.shape)


def attend_forward(proj, seq):
    rows, width = proj.shape[0], proj.shape[1] // 3
    group = width // IMAGES
    lanes = max(LANES, group)
    steps = width // lanes

    return pl.pallas_call(
        functools.partial(attend_kernel, seq, group),
        grid=(steps,),
        in_specs=[pl.BlockSpec((rows, 3 * lanes), lambda i: (0, i))],
        out_specs=pl.BlockSpec((rows, lanes), lambda i: (0, i)),
        out_shape=jax.ShapeDtypeStruct((rows, width), LOW),
        compiler_params=pltpu.CompilerParams(vmem_limit_bytes=32 << 20),
        cost_estimate=pl.CostEstimate(
            flops=8 * rows * rows * width,
            bytes_accessed=8 * rows * width,
            transcendentals=rows * rows * width // HEAD,
        ),
    )(proj)


def attend_backward(proj, out, d_out, seq):
    rows, width = out.shape
    group = width // IMAGES
    lanes = max(LANES, group)
    steps = width // lanes

    sums = pl.BlockSpec((8, lanes), lambda i: (0, i))
    column = pl.BlockSpec((rows, lanes), lambda i: (0, i))
    triple = pl.BlockSpec((rows, 3 * lanes), lambda i: (0, i))
    low = jax.ShapeDtypeStruct((rows, 3 * width), LOW)
    wide = jax.ShapeDtypeStruct((8, width), WIDE)
    return pl.pallas_call(
        functools.partial(attend_back_kernel, seq, group),
        grid=(steps,),
        in_specs=[triple, column, column],
        out_specs=[triple, sums, sums],
        out_shape=[low, wide, wide],
        compiler_params=pltpu.CompilerParams(vmem_limit_bytes=32 << 20),
        cost_estimate=pl.CostEstimate(
            flops=20 * rows * rows * width,
            bytes_accessed=16 * rows * width,
            transcendentals=rows * rows * width // HEAD,
        ),
    )(proj, out, d_out)


def adam_update(param, gradient, moments, decay):
    first = BETA_ONE * moments[0] + (1.0 - BETA_ONE) * gradient
    second = BETA_TWO * moments[1] + (1.0 - BETA_TWO) * gradient * gradient
    fix_one = 1.0 - BETA_ONE**STEP
    fix_two = 1.0 - BETA_TWO**STEP
    update = first / fix_one / (jnp.sqrt(second / fix_two) + ADAM_EPS) + decay * param
    return (param - LEARN_RATE * update, jnp.stack([first, second]))


def on_device(
    tokens,
    cotangent,
    image_counts,
    w_qkv,
    w_out,
    w_fc1,
    w_fc2,
    vec_small,
    fc1_bias,
    mom_qkv,
    mom_out,
    mom_fc1,
    mom_fc2,
    mom_vec,
    mom_bias,
):
    core, img, sub = lax.axis_index("core"), lax.axis_index("img"), lax.axis_index("sub")
    subs = lax.axis_size("sub")
    layers, rows = w_qkv.shape[0], w_qkv.shape[1]
    seq, feat = tokens.shape[1], tokens.shape[2]
    width = feat * IMAGES * subs
    hidden = fc1_bias.shape[1]
    padded = -(-seq // 16) * 16
    slot_live = jnp.stack([jnp.ones((), WIDE), (image_counts[0] == 2).astype(WIDE)])[:, None, None]

    def pad(image):
        return jnp.pad(image, ((0, padded - seq), (0, 0)))

    inner = IMAGES * feat // 2
    kinds = (3, 1, 1, 1)
    shards = [
        w[n].reshape(rows, -1).astype(LOW)
        for n in range(layers)
        for w in (w_qkv, w_out, w_fc1, w_fc2)
    ]
    gathered = gather_weights(shards, kinds * layers)
    weights = [[gathered[4 * n + k] for k in range(4)] for n in range(layers)]

    state = pad(to_images(tokens)).astype(WIDE)

    vec_rows = vec_small.shape[0] * vec_small.shape[1]
    small = jnp.concatenate(
        [vec_small.reshape(vec_rows, feat), fc1_bias.reshape(-1, feat)], axis=0
    )
    for bit in bits_of("sub"):
        small = gather_step(small.reshape((-1, 1) + small.shape[-2:]), "sub", bit)
    small = small.reshape((subs,) + small.shape[-2:])
    small = jnp.stack(line_in_order(small, "img"))
    vec_near = small[:, :, :vec_rows].reshape(
        (IMAGES, subs, vec_small.shape[0], vec_small.shape[1], feat)
    ).transpose(2, 3, 0, 1, 4)
    bias_near = small[:, :, vec_rows:].reshape(IMAGES, subs, layers, hidden).transpose(2, 0, 1, 3)

    def own_half(blocks_of):
        n = blocks_of.shape[-1] // 2
        lead = blocks_of.shape[:-3]
        cut = blocks_of.reshape(lead + (IMAGES, subs, 2, n))
        cut = lax.dynamic_index_in_dim(cut, sub, len(lead) + 1, keepdims=False)
        cut = lax.dynamic_index_in_dim(cut, core, len(lead) + 1, keepdims=False)
        return cut.reshape(lead + (IMAGES * n,))

    vec_half = own_half(vec_near)
    bias_half = own_half(bias_near)
    vec_full = vec_near.reshape(vec_small.shape[:2] + (width,))

    cotangent, weights[0][0] = lax.optimization_barrier((cotangent, weights[0][0]))
    gradient = to_images((cotangent * slot_live).astype(LOW))

    saved = []
    for n in range(layers):
        qkv_weight, out_weight, first_weight, second_weight = weights[n]
        full = vec_full[n]
        hat_one, inv_one = norm_forward(state)
        normed_one = (hat_one * full[0] + full[1]).astype(LOW)
        shift = jnp.stack([vec_half[n, 2], jnp.zeros_like(vec_half[n, 2]), vec_half[n, 3]])
        shift = shift.reshape(3, IMAGES, -1).transpose(1, 0, 2).reshape(-1)
        proj = (dot(normed_one, qkv_weight) + shift).astype(LOW)
        attended = attend_forward(proj, seq)
        middle = state + group_sum(dot(attended, out_weight, CONTRACT_LAST)) + full[4]
        hat_two, inv_two = norm_forward(middle)
        normed_two = (hat_two * full[5] + full[6]).astype(LOW)
        before = dot(normed_two, first_weight) + bias_half[n]
        active = (before * gelu_parts(before)).astype(LOW)
        branch = dot(active, second_weight, CONTRACT_LAST)
        saved.append(
            (hat_one, inv_one, normed_one, proj, attended, hat_two, inv_two, normed_two, before, active)
        )
        if n == 0:
            gradient, branch = lax.optimization_barrier((gradient, branch))
        state = middle + group_sum(branch) + full[7]
    output = from_images(state[:seq].astype(LOW)).astype(WIDE) * slot_live

    gradient = pad(gradient).astype(WIDE)
    big = [None] * layers
    small_grads = [None] * layers
    for n in reversed(range(layers)):
        qkv_weight, out_weight, first_weight, second_weight = weights[n]
        full = vec_full[n]
        (hat_one, inv_one, normed_one, proj, attended, hat_two, inv_two, normed_two, before, active) = saved[n]
        grad_low = gradient.astype(LOW)
        g_second = dot(grad_low, active, CONTRACT_FIRST).astype(LOW)
        g_last = jnp.sum(gradient, 0)
        slope = gelu_parts(before) + before * jnp.exp(-0.5 * before * before) * INV_ROOT_TWO_PI
        d_before = dot(grad_low, second_weight) * slope
        d_low = d_before.astype(LOW)
        if n:
            g_second, d_low = lax.optimization_barrier((g_second, d_low))
        g_bias = jnp.sum(d_before, 0)
        g_first = dot(normed_two, d_low, CONTRACT_FIRST).astype(LOW)
        d_normed = group_sum(dot(d_low, first_weight, CONTRACT_LAST))
        middle_grad, g_gain_two, g_shift_two = norm_backward(
            d_normed, hat_two, inv_two, full[5], gradient
        )
        mid_low = middle_grad.astype(LOW)
        g_out_bias = jnp.sum(middle_grad, 0)
        g_out = dot(mid_low, attended, CONTRACT_FIRST).astype(LOW)
        d_attended = dot(mid_low, out_weight).astype(LOW)
        d_proj, sum_query, sum_value = attend_backward(proj, attended, d_attended, seq)
        g_qkv = dot(normed_one, d_proj, CONTRACT_FIRST).astype(LOW)
        d_normed = group_sum(dot(d_proj, qkv_weight, CONTRACT_LAST))
        gradient, g_gain_one, g_shift_one = norm_backward(
            d_normed, hat_one, inv_one, full[0], middle_grad
        )
        big[n] = [g_second, g_first, g_out, g_qkv]
        of_features = jnp.stack(
            [g_gain_one, g_shift_one, g_out_bias, g_gain_two, g_shift_two, g_last]
        )
        small_grads[n] = jnp.concatenate(
            [of_features.reshape(-1), sum_query[0], sum_value[0], g_bias]
        ).reshape(-1, LANES)
        if n:
            big[n][0] = scatter_plain(g_second, 1)
    small_total = jnp.stack(small_grads)
    sent_back = gradient[:seq].astype(LOW)
    small_total, sent_back, big[0][-1] = lax.optimization_barrier(
        (small_total, sent_back, big[0][-1])
    )
    small_total = chip_sum(small_total)
    sent_back = from_images(sent_back)
    order = [(n, 1) for n in range(1, layers)] + [(n, 3) for n in range(1, layers)]
    order += [(0, 0), (0, 1)] + [(n, 2) for n in range(1, layers)] + [(0, 2), (0, 3)]
    summed = scatter_grads([big[n][k] for n, k in order], [(1, 1, 1, 3)[k] for _, k in order])
    for (n, k), total in zip(order, summed):
        big[n][k] = total
    input_grad = sent_back.astype(WIDE) * slot_live
    big = [b[::-1] for b in big]

    grads = [
        [big[n][k].reshape(w.shape[1:]) for n in range(layers)]
        for k, w in enumerate((w_qkv, w_out, w_fc1, w_fc2))
    ]

    vec_rows_of = []
    bias_rows_of = []
    for n in range(layers):
        total = small_total[n].reshape(-1)
        whole = total[: 6 * width].reshape(6, IMAGES, subs, feat)
        whole = lax.dynamic_index_in_dim(whole, img, 1, keepdims=False)
        whole = lax.dynamic_index_in_dim(whole, sub, 1, keepdims=False)
        split = total[6 * width : 6 * width + 2 * inner].reshape(2, IMAGES, feat // 2)
        split = lax.dynamic_index_in_dim(split, img, 1, keepdims=False)
        fc = total[6 * width + 2 * inner :].reshape(IMAGES, hidden // 2)
        fc = lax.dynamic_index_in_dim(fc, img, 0, keepdims=False)
        mine = jnp.concatenate([split.reshape(-1), fc])
        pair = gather_step(mine.reshape(-1, LANES // 2), "core", 1).reshape(2, -1)
        split = pair[:, :feat].reshape(2, 2, feat // 2).transpose(1, 0, 2).reshape(2, feat)
        vec_rows_of.append(
            jnp.stack(
                [whole[0], whole[1], split[0], split[1], whole[2], whole[3], whole[4], whole[5]]
            )
        )
        bias_rows_of.append(pair[:, feat:].reshape(-1))

    totals = tuple(jnp.stack(g) for g in grads) + (jnp.stack(vec_rows_of), jnp.stack(bias_rows_of))
    params = (w_qkv, w_out, w_fc1, w_fc2, vec_small, fc1_bias)
    moments = (mom_qkv, mom_out, mom_fc1, mom_fc2, mom_vec, mom_bias)
    decays = (WEIGHT_DECAY, WEIGHT_DECAY, WEIGHT_DECAY, WEIGHT_DECAY, 0.0, 0.0)
    results = [
        adam_update(param, total, moment, decay)
        for param, total, moment, decay in zip(params, totals, moments, decays)
    ]
    return (
        (output, input_grad)
        + totals
        + tuple(r[0] for r in results)
        + tuple(r[1] for r in results)
    )


def solution(mesh):
    dp, tensor = mesh.shape["dp"], mesh.shape["tensor"]
    inner = Mesh(
        mesh.devices.reshape(dp // 2, 2, IMAGES, tensor // IMAGES), ("pos", "core", "img", "sub")
    )
    rows, cols = ("pos", "core"), ("img", "sub")
    images = P(rows, None, cols)
    weight = [P(None, rows, None, cols)] + [P(None, rows, cols)] * 3
    moment = [P(None, None, rows, None, cols)] + [P(None, None, rows, cols)] * 3
    vector = [P(None, None, cols), P(None, cols)]
    moment_vector = [P(None, None, None, cols), P(None, None, cols)]
    return jax.shard_map(
        on_device,
        mesh=inner,
        in_specs=tuple([images, images, P(rows)] + weight + vector + moment + moment_vector),
        out_specs=tuple(
            [images, images] + weight + vector + weight + vector + moment + moment_vector
        ),
        check_vma=False,
    )
```

```python
import functools

import jax
import jax.numpy as jnp
from jax import lax
from jax.experimental import pallas as pl
from jax.experimental.pallas import tpu as pltpu
from jax.sharding import Mesh, PartitionSpec as P

HEAD = 64
STEP = 10
IMAGES = 4

NORM_EPS = 1e-06
ROOT_HALF = 0.7071067811865476
INV_ROOT_TWO_PI = 0.3989422804014327
LEARN_RATE = 0.01
BETA_ONE = 0.9
BETA_TWO = 0.999
ADAM_EPS = 1e-08
WEIGHT_DECAY = 0.05
CONTRACT_LAST = (((1,), (1,)), ((), ()))
CONTRACT_FIRST = (((0,), (0,)), ((), ()))
LOW = jnp.bfloat16
WIDE = jnp.float32
LANES = 128


def dot(left, right, dims=(((1,), (0,)), ((), ()))):
    return lax.dot_general(left, right, dims, preferred_element_type=WIDE)


def bits_of(axis):
    count = lax.axis_size(axis)
    return [1 << i for i in range(count.bit_length() - 1)]


def swap(value, axis, bit):
    count = lax.axis_size(axis)
    return lax.ppermute(value, axis, [(i, i ^ bit) for i in range(count)])


def bit_set(axis, bit):
    return (lax.axis_index(axis) // bit) % 2 == 1


def in_order(mine, arrived, axis, bit):
    upper = bit_set(axis, bit)
    return jnp.stack([jnp.where(upper, arrived, mine), jnp.where(upper, mine, arrived)])


def gather_step(mine, axis, bit):
    return in_order(mine, swap(mine, axis, bit), axis, bit)


def untangle(pieces, axis):
    for bit in bits_of(axis):
        upper = bit_set(axis, bit)
        pieces = [jnp.where(upper, pieces[d ^ bit], pieces[d]) for d in range(len(pieces))]
    return pieces


def line_in_order(value, axis):
    return untangle(
        [swap(value, axis, d) if d else value for d in range(lax.axis_size(axis))], axis
    )


MESH = pl.DeviceIdType.MESH


def greet(partners):
    barrier = pltpu.get_barrier_semaphore()
    for partner in partners:
        pl.semaphore_signal(barrier, inc=1, device_id=partner, device_id_type=MESH)
    pl.semaphore_wait(barrier, len(partners))


def partners_of(count):
    pos, img = lax.axis_index("pos"), lax.axis_index("img")
    bits = [1 << i for i in range(count.bit_length() - 1)]
    twin = [{"core": 1 - lax.axis_index("core")}]
    return twin + [{"img": img ^ d} for d in range(1, IMAGES)] + [{"pos": pos ^ b} for b in bits]


def sends_of(count):
    bits = [1 << i for i in range(count.bit_length() - 1)]
    table = []
    for which, order in enumerate((bits, bits[::-1])):
        held = [0]
        for stage, bit in enumerate(order):
            table += [(which, stage, bit, d) for d in held]
            held = held + [d | bit for d in held]
    return table


def gather_kernel(count, kinds, *refs):
    pieces = len(kinds)
    shards, wholes = refs[:pieces], refs[pieces : 2 * pieces]
    own_sem, twin_send, twin_recv, near_send, near_recv, far_send, far_recv = refs[2 * pieces :]
    pos, img, core = lax.axis_index("pos"), lax.axis_index("img"), lax.axis_index("core")
    half_rows = shards[0].shape[0]
    rows = 2 * half_rows
    table = sends_of(count)
    greet(partners_of(count))

    def place(p, q, first, blocks_wide):
        cols = shards[p].shape[1] // 2
        return wholes[p].at[
            pl.ds(pl.multiple_of(q * rows, rows), rows),
            pl.ds(pl.multiple_of(first * cols, cols), blocks_wide * cols),
        ]

    own, twin, near, far = {}, {}, {}, {}
    for p in range(pieces):
        share = shards[p].shape[1] // (2 * kinds[p])
        for k in range(kinds[p]):
            first = (img * kinds[p] + k) * share
            there = wholes[p].at[
                pl.ds(pl.multiple_of(pos * rows + core * half_rows, half_rows), half_rows),
                pl.ds(pl.multiple_of(first, share), share),
            ]

            def columns(which, p=p, k=k, share=share):
                return shards[p].at[:, pl.ds(pl.multiple_of((2 * k + which) * share, share), share)]

            twin[p, k] = pltpu.make_async_remote_copy(
                src_ref=columns(1 - core),
                dst_ref=there,
                send_sem=twin_send.at[p, k],
                recv_sem=twin_recv.at[p, k],
                device_id={"core": 1 - core},
                device_id_type=MESH,
            )
            twin[p, k].start()
            own[p, k] = pltpu.make_async_copy(columns(core), there, own_sem.at[p, k])
            own[p, k].start()

    def start_near(p):
        for k in range(kinds[p]):
            own[p, k].wait()
            twin[p, k].wait_recv()
        for d in range(1, IMAGES):
            near[p, d] = pltpu.make_async_remote_copy(
                src_ref=place(p, pos, img, 1),
                dst_ref=place(p, pos, img, 1),
                send_sem=near_send.at[p, d],
                recv_sem=near_recv.at[p, d],
                device_id={"img": img ^ d},
                device_id_type=MESH,
            )
            near[p, d].start()

    def start(p, entries):
        for e in entries:
            which, stage, bit, offset = table[e]
            there = place(p, pos ^ offset, which * (IMAGES // 2), IMAGES // 2)
            far[p, e] = pltpu.make_async_remote_copy(
                src_ref=there,
                dst_ref=there,
                send_sem=far_send.at[p, e],
                recv_sem=far_recv.at[p, e],
                device_id={"pos": pos ^ bit},
                device_id_type=MESH,
            )
            far[p, e].start()

    def forward(p):
        for e, (which, stage, bit, offset) in enumerate(table):
            if offset:
                last = max(
                    (f for f, t in enumerate(table) if t[0] == which and offset & t[2]),
                    key=lambda f: table[f][1],
                )
                source = next(
                    f
                    for f, t in enumerate(table)
                    if t[0] == which and t[2] == table[last][2] and t[3] == offset ^ table[last][2]
                )
                if (p, source) not in landed:
                    far[p, source].wait_recv()
                    landed.add((p, source))
                start(p, [e])

    landed = set()
    for p in range(min(AHEAD, pieces)):
        start_near(p)
    for p in range(pieces):
        if p + AHEAD < pieces:
            start_near(p + AHEAD)
        for d in range(1, IMAGES):
            near[p, d].wait_recv()
        start(p, [e for e, t in enumerate(table) if t[3] == 0])
        if p:
            forward(p - 1)
    forward(pieces - 1)
    for p in range(pieces):
        for k in range(kinds[p]):
            twin[p, k].wait_send()
        for d in range(1, IMAGES):
            near[p, d].wait_send()
        for e in range(len(table)):
            if (p, e) not in landed:
                far[p, e].wait_recv()
            far[p, e].wait_send()


def cut_halves(shard, kinds):
    pair = shard.reshape(shard.shape[0], kinds, 2, -1)
    return [pair[:, :, which].reshape(shard.shape[0], -1) for which in range(2)]


def gather_plain(shard, kinds):
    core = lax.axis_index("core")
    pair = cut_halves(shard, kinds)
    kept = jnp.where(core == 1, pair[1], pair[0])
    sent = jnp.where(core == 1, pair[0], pair[1])
    block = in_order(kept, swap(sent, "core", 1), "core", 1).reshape(2 * shard.shape[0], -1)
    whole = lax.all_gather(block, ("img", "pos")).reshape(IMAGES, -1, block.shape[1])
    return jnp.concatenate([whole[i] for i in range(IMAGES)], axis=1)


def scatter_plain(grad, kinds):
    core, count = lax.axis_index("core"), lax.axis_size("pos")
    parts = jnp.stack(jnp.split(grad, IMAGES, axis=1))
    parts = parts.reshape(IMAGES * count, grad.shape[0] // count, -1)
    block = lax.psum_scatter(parts, ("img", "pos")).astype(WIDE)
    block = block.reshape(2, block.shape[0] // 2, -1)
    kept = jnp.where(core == 1, block[1], block[0])
    sent = jnp.where(core == 1, block[0], block[1]).astype(LOW)
    both = in_order(kept, swap(sent, "core", 1).astype(WIDE), "core", 1)
    both = both.reshape(2, both.shape[1], kinds, -1).transpose(1, 2, 0, 3)
    return both.reshape(both.shape[0], -1)


def aligned(width, kinds):
    return width // (2 * kinds) % LANES == 0


def gather_weights(shards, kinds):
    if not all(aligned(w.shape[1], k) for w, k in zip(shards, kinds)):
        good = [i for i, w in enumerate(shards) if aligned(w.shape[1], kinds[i])]
        done = dict(zip(good, gather_weights([shards[i] for i in good], [kinds[i] for i in good])))
        return [
            done[i] if i in done else gather_plain(w, kinds[i]) for i, w in enumerate(shards)
        ]
    count, pieces = lax.axis_size("pos"), len(shards)
    copies, most = len(sends_of(count)), max(kinds)
    moved = sum(2 * count * IMAGES * w.size for w in shards)
    anywhere = pl.BlockSpec(memory_space=pl.ANY)
    return pl.pallas_call(
        functools.partial(gather_kernel, count, tuple(kinds)),
        in_specs=[anywhere] * pieces,
        out_specs=[anywhere] * pieces,
        out_shape=[
            jax.ShapeDtypeStruct((count * 2 * w.shape[0], IMAGES * w.shape[1] // 2), LOW)
            for w in shards
        ],
        scratch_shapes=[
            pltpu.SemaphoreType.DMA((pieces, most)),
            pltpu.SemaphoreType.DMA((pieces, most)),
            pltpu.SemaphoreType.DMA((pieces, most)),
            pltpu.SemaphoreType.DMA((pieces, IMAGES)),
            pltpu.SemaphoreType.DMA((pieces, IMAGES)),
            pltpu.SemaphoreType.DMA((pieces, copies)),
            pltpu.SemaphoreType.DMA((pieces, copies)),
        ],
        compiler_params=pltpu.CompilerParams(collective_id=0, has_side_effects=True),
        cost_estimate=pl.CostEstimate(flops=0, bytes_accessed=8 * moved, transcendentals=0),
    )(*shards)


def receipts_of(count):
    bits = [1 << i for i in range(count.bit_length() - 1)]
    table = []
    for which, order in enumerate((bits[::-1], bits)):
        kept = list(range(count))
        for stage, bit in enumerate(order):
            kept = [d for d in kept if not d & bit]
            table += [(which, stage, bit, d) for d in kept]
    return table


CHUNK = 32
AHEAD = 1


def scatter_kernel(count, kinds, *refs):
    pieces = len(kinds)
    grads, small, refs = refs[:pieces], refs[pieces], refs[pieces + 1 :]
    outs, small_out, refs = refs[:pieces], refs[pieces], refs[pieces + 1 :]
    arrived, sums, near, gone, come = [refs[i * pieces : (i + 1) * pieces] for i in range(5)]
    far_send, far_recv, near_send, near_recv, twin_send, twin_recv = refs[5 * pieces : -4]
    small_sum, small_in, small_send, small_recv = refs[-4:]
    pos, img, core = lax.axis_index("pos"), lax.axis_index("img"), lax.axis_index("core")
    half_rows = outs[0].shape[0]
    rows = 2 * half_rows
    table = receipts_of(count)
    stages = max(t[1] for t in table) + 1
    half = IMAGES // 2
    greet(partners_of(count))
    far, close, twin = {}, {}, {}

    partial = {}

    def whole_part(p, which, offset):
        cols = outs[p].shape[1] // 2
        return grads[p].at[
            pl.ds(pl.multiple_of((pos ^ offset) * rows, rows), rows),
            pl.ds(which * half * cols, half * cols),
        ]

    def send(p, stage):
        for e, (which, at, bit, offset) in enumerate(table):
            if at == stage:
                far[p, e] = pltpu.make_async_remote_copy(
                    src_ref=partial[p, which, offset | bit]
                    if stage
                    else whole_part(p, which, offset | bit),
                    dst_ref=arrived[p].at[e],
                    send_sem=far_send.at[p, e],
                    recv_sem=far_recv.at[p, e],
                    device_id={"pos": pos ^ bit},
                    device_id_type=MESH,
                )
                far[p, e].start()

    def add(p, stage):
        for e, (which, at, bit, offset) in enumerate(table):
            if at != stage:
                continue
            far[p, e].wait_recv()
            cols = outs[p].shape[1] // 2
            before = partial[p, which, offset] if stage else whole_part(p, which, offset)
            slot = arrived[p].at[e]

            def body(i, carry, before=before, slot=slot, which=which, p=p, cols=cols):
                step = pl.ds(pl.multiple_of(i * CHUNK, CHUNK), CHUNK)
                total = (before[step, :].astype(WIDE) + slot[step, :].astype(WIDE)).astype(LOW)
                if stage < stages - 1:
                    slot[step, :] = total
                else:
                    for j in range(half):
                        sums[p][which * half + j, step] = total[:, j * cols : (j + 1) * cols]
                return carry

            lax.fori_loop(0, rows // CHUNK, body, 0)
            partial[p, which, offset] = slot

    def send_near(p):
        for d in range(1, IMAGES):
            close[p, d] = pltpu.make_async_remote_copy(
                src_ref=sums[p].at[img ^ d],
                dst_ref=near[p].at[d - 1],
                send_sem=near_send.at[p, d],
                recv_sem=near_recv.at[p, d],
                device_id={"img": img ^ d},
                device_id_type=MESH,
            )
            close[p, d].start()

    def columns(p, k, which):
        share = outs[p].shape[1] // (2 * kinds[p])
        return pl.ds(pl.multiple_of((2 * k + which) * share, share), share)

    def finish(p):
        share = outs[p].shape[1] // (2 * kinds[p])
        for d in range(1, IMAGES):
            close[p, d].wait_recv()

        def total_of(first):
            step = pl.ds(pl.multiple_of(first, CHUNK), CHUNK)
            total = sums[p][img, step].astype(WIDE)
            for d in range(1, IMAGES):
                total += near[p][d - 1, step].astype(WIDE)
            return total

        def other(i, carry):
            step = pl.ds(pl.multiple_of(i * CHUNK, CHUNK), CHUNK)
            gone[p][step, :] = total_of((1 - core) * half_rows + i * CHUNK).astype(LOW)
            return carry

        lax.fori_loop(0, half_rows // CHUNK, other, 0)
        twin[p] = pltpu.make_async_remote_copy(
            src_ref=gone[p],
            dst_ref=come[p],
            send_sem=twin_send.at[p],
            recv_sem=twin_recv.at[p],
            device_id={"core": 1 - core},
            device_id_type=MESH,
        )
        twin[p].start()

        def mine(i, carry):
            step = pl.ds(pl.multiple_of(i * CHUNK, CHUNK), CHUNK)
            total = total_of(core * half_rows + i * CHUNK)
            for k in range(kinds[p]):
                outs[p][step, columns(p, k, core)] = total[:, k * share : (k + 1) * share]
            return carry

        lax.fori_loop(0, half_rows // CHUNK, mine, 0)

    def close_twin(p):
        share = outs[p].shape[1] // (2 * kinds[p])
        twin[p].wait_recv()

        def body(i, carry):
            step = pl.ds(pl.multiple_of(i * CHUNK, CHUNK), CHUNK)
            total = come[p][step, :].astype(WIDE)
            for k in range(kinds[p]):
                outs[p][step, columns(p, k, 1 - core)] = total[:, k * share : (k + 1) * share]
            return carry

        lax.fori_loop(0, half_rows // CHUNK, body, 0)

    steps = [("img", 1), ("img", 2)] + [("pos", 1 << i) for i in range(stages)] + [("core", 1)]
    passed = {}

    def small_step(turn):
        if 0 < turn <= len(steps):
            passed[turn - 1].wait_recv()
        if turn < len(steps):
            before = small if turn == 0 else small_sum.at[turn - 1]
            small_sum[turn] = small[...] if turn == 0 else before[...] + small_in[turn - 1]
            axis, bit = steps[turn]
            passed[turn] = pltpu.make_async_remote_copy(
                src_ref=small_sum.at[turn],
                dst_ref=small_in.at[turn],
                send_sem=small_send.at[turn],
                recv_sem=small_recv.at[turn],
                device_id={axis: lax.axis_index(axis) ^ bit},
                device_id_type=MESH,
            )
            passed[turn].start()
        if turn == len(steps):
            small_out[0] = small_sum[turn - 1]
            small_out[1] = small_in[turn - 1]

    turns = max(pieces + stages + 2, len(steps) + 1)
    for turn in range(turns):
        if turn < pieces:
            send(turn, 0)
        small_step(turn)
        for stage in range(stages):
            p = turn - 1 - stage
            if 0 <= p < pieces:
                add(p, stage)
                if stage < stages - 1:
                    send(p, stage + 1)
                else:
                    send_near(p)
        p = turn - 1 - stages
        if 0 <= p < pieces:
            finish(p)
        p -= 1
        if 0 <= p < pieces:
            close_twin(p)
    for turn in range(len(steps)):
        passed[turn].wait_send()
    for p in range(pieces):
        twin[p].wait_send()
        for e in range(len(table)):
            far[p, e].wait_send()
        for d in range(1, IMAGES):
            close[p, d].wait_send()


def scatter_grads(grads, kinds, small):
    widths = [2 * g.shape[1] // IMAGES for g in grads]
    if not all(aligned(w, k) for w, k in zip(widths, kinds)):
        good = [i for i, w in enumerate(widths) if aligned(w, kinds[i])]
        summed, small = scatter_grads([grads[i] for i in good], [kinds[i] for i in good], small)
        done = dict(zip(good, summed))
        every = [done[i] if i in done else scatter_plain(g, kinds[i]) for i, g in enumerate(grads)]
        return every, small
    count, pieces = lax.axis_size("pos"), len(grads)
    copies = len(receipts_of(count))
    shapes = [(g.shape[0] // count, g.shape[1] // IMAGES) for g in grads]
    in_vmem = pl.BlockSpec(memory_space=pltpu.VMEM)
    moved = sum(2 * g.size for g in grads)
    steps = count.bit_length() - 1 + 3
    out = pl.pallas_call(
        functools.partial(scatter_kernel, count, tuple(kinds)),
        in_specs=[in_vmem] * (pieces + 1),
        out_specs=[in_vmem] * (pieces + 1),
        out_shape=[jax.ShapeDtypeStruct((r // 2, 2 * c), WIDE) for r, c in shapes]
        + [jax.ShapeDtypeStruct((2,) + small.shape, WIDE)],
        scratch_shapes=[pltpu.VMEM((copies, r, IMAGES // 2 * c), LOW) for r, c in shapes]
        + [pltpu.VMEM((IMAGES, r, c), LOW) for r, c in shapes]
        + [pltpu.VMEM((IMAGES - 1, r, c), LOW) for r, c in shapes]
        + [pltpu.VMEM((r // 2, c), LOW) for r, c in shapes]
        + [pltpu.VMEM((r // 2, c), LOW) for r, c in shapes]
        + [
            pltpu.SemaphoreType.DMA((pieces, copies)),
            pltpu.SemaphoreType.DMA((pieces, copies)),
            pltpu.SemaphoreType.DMA((pieces, IMAGES)),
            pltpu.SemaphoreType.DMA((pieces, IMAGES)),
            pltpu.SemaphoreType.DMA((pieces,)),
            pltpu.SemaphoreType.DMA((pieces,)),
            pltpu.VMEM((steps,) + small.shape, WIDE),
            pltpu.VMEM((steps,) + small.shape, WIDE),
            pltpu.SemaphoreType.DMA((steps,)),
            pltpu.SemaphoreType.DMA((steps,)),
        ],
        compiler_params=pltpu.CompilerParams(
            collective_id=1, has_side_effects=True, vmem_limit_bytes=48 << 20
        ),
        cost_estimate=pl.CostEstimate(flops=0, bytes_accessed=8 * moved, transcendentals=0),
    )(*grads, small)
    return list(out[:-1]), out[-1]


def group_sum(partial):
    for axis in ("core", "sub"):
        for bit in bits_of(axis):
            partial = partial + swap(partial.astype(LOW), axis, bit).astype(WIDE)
    return partial


def send_column(value, distance):
    return lax.ppermute(value, ("core", "img"), distance)


def to_images(slots, after):
    core, img = lax.axis_index("core"), lax.axis_index("img")
    pieces = []
    for distance in range(IMAGES):
        payload = jnp.where((img ^ distance) % 2 == 1, slots[1], slots[0])
        if distance:
            pairs = [
                (c * IMAGES + (i ^ distance), c * IMAGES + i)
                for c in range(2)
                for i in range(IMAGES)
                if i // 2 == c
            ]
            payload = send_column(payload, pairs)
        pieces.append(payload)
    pieces, after = lax.optimization_barrier((pieces, after))
    pieces = untangle(pieces, "img")
    for bit in bits_of("sub"):
        pieces = [
            jnp.concatenate(list(gather_step(p, "sub", bit)), axis=-1) for p in pieces
        ]
    mine = jnp.concatenate(pieces, axis=-1)
    return jnp.where(img // 2 == core, mine, swap(mine, "core", 1))


def from_images(image):
    core, img, sub = lax.axis_index("core"), lax.axis_index("img"), lax.axis_index("sub")
    seq, width = image.shape
    subs = lax.axis_size("sub")
    share = width // (IMAGES * subs)
    image = image.reshape(seq, IMAGES, subs, share)
    if subs > 1:
        image = lax.dynamic_index_in_dim(image, sub, 2, keepdims=True)
    blocks = [image[:, i, 0] for i in range(IMAGES)]
    blocks = untangle(blocks, "img")
    pieces = [blocks[0]]
    for distance in range(1, IMAGES):
        pairs = [
            (c * IMAGES + i, c * IMAGES + (i ^ distance))
            for c in range(2)
            for i in range(IMAGES)
            if i // 2 == c
        ]
        pieces.append(send_column(blocks[distance], pairs))
    pieces = untangle(pieces, "img")
    return jnp.stack([jnp.where(core == 1, pieces[2 + s], pieces[s]) for s in range(2)])


def gelu_parts(value):
    return 0.5 * (1.0 + lax.erf(value * ROOT_HALF))


def norm_forward(hidden):
    mean = jnp.mean(hidden, -1, keepdims=True)
    spread = jnp.mean(hidden * hidden, -1, keepdims=True) - mean * mean
    inv = lax.rsqrt(spread + NORM_EPS)
    return (hidden - mean) * inv, inv


def norm_backward(d_normed, normed, inv, gain, carried):
    d_hat = d_normed * gain
    plain = jnp.mean(d_hat, -1, keepdims=True)
    crossed = jnp.mean(d_hat * normed, -1, keepdims=True)
    grad = carried + inv * (d_hat - plain - normed * crossed)
    return grad, jnp.sum(d_normed * normed, 0), jnp.sum(d_normed, 0)


def softmax_rows(query, key, seq):
    scores = dot(query, key, CONTRACT_LAST) * HEAD ** (-0.5)
    column = lax.broadcasted_iota(jnp.int32, scores.shape, 1)
    scores = jnp.where(column < seq, scores, -1e30)
    raised = jnp.exp(scores - jnp.max(scores, -1, keepdims=True))
    return raised * (1.0 / jnp.sum(raised, -1, keepdims=True))


def split_three(value, group):
    cuts = [value[:, i : i + group] for i in range(0, value.shape[1], group)]
    if len(cuts) == 3:
        return cuts
    return [jnp.concatenate(cuts[k::3], axis=1) for k in range(3)]


def attend_kernel(seq, group, proj_ref, o_ref):
    query, key, value = split_three(proj_ref[...], group)
    lane_head = lax.broadcasted_iota(jnp.int32, query.shape, 1) // HEAD
    total = jnp.zeros(query.shape, WIDE)
    for head in range(query.shape[1] // HEAD):
        own = lane_head == head
        probs = softmax_rows(jnp.where(own, query, jnp.zeros_like(query)), key, seq)
        total = jnp.where(own, dot(probs.astype(LOW), value), total)
    o_ref[...] = total.astype(LOW)


def attend_back_kernel(seq, group, proj_ref, o_ref, do_ref, dproj_ref, sq_ref, sv_ref):
    query, key, value = split_three(proj_ref[...], group)
    out, d_out = o_ref[...].astype(WIDE), do_ref[...]
    lane_head = lax.broadcasted_iota(jnp.int32, query.shape, 1) // HEAD
    d_query = jnp.zeros(query.shape, WIDE)
    d_key = jnp.zeros(query.shape, WIDE)
    d_value = jnp.zeros(query.shape, WIDE)
    for head in range(query.shape[1] // HEAD):
        own = lane_head == head
        probs = softmax_rows(jnp.where(own, query, jnp.zeros_like(query)), key, seq)
        d_own = jnp.where(own, d_out, jnp.zeros_like(d_out))
        d_value = jnp.where(own, dot(probs.astype(LOW), d_out, CONTRACT_FIRST), d_value)
        d_probs = dot(d_own, value, CONTRACT_LAST)
        delta = jnp.sum(d_own.astype(WIDE) * out, -1, keepdims=True)
        d_scores = (probs * (d_probs - delta) * HEAD ** (-0.5)).astype(LOW)
        d_query = jnp.where(own, dot(d_scores, key), d_query)
        d_key = jnp.where(own, dot(d_scores, query, CONTRACT_FIRST), d_key)
    for which, part in enumerate((d_query, d_key, d_value)):
        for j in range(part.shape[1] // group):
            at = (3 * j + which) * group
            dproj_ref[:, at : at + group] = part[:, j * group : (j + 1) * group].astype(LOW)
    sq_ref[...] = jnp.broadcast_to(jnp.sum(d_query, 0, keepdims=True), sq_ref.shape)
    sv_ref[...] = jnp.broadcast_to(jnp.sum(d_value, 0, keepdims=True), sv_ref.shape)


def attend_forward(proj, seq):
    rows, width = proj.shape[0], proj.shape[1] // 3
    group = width // IMAGES
    lanes = max(LANES, group)
    steps = width // lanes

    return pl.pallas_call(
        functools.partial(attend_kernel, seq, group),
        grid=(steps,),
        in_specs=[pl.BlockSpec((rows, 3 * lanes), lambda i: (0, i))],
        out_specs=pl.BlockSpec((rows, lanes), lambda i: (0, i)),
        out_shape=jax.ShapeDtypeStruct((rows, width), LOW),
        compiler_params=pltpu.CompilerParams(vmem_limit_bytes=32 << 20),
        cost_estimate=pl.CostEstimate(
            flops=8 * rows * rows * width,
            bytes_accessed=8 * rows * width,
            transcendentals=rows * rows * width // HEAD,
        ),
    )(proj)


def attend_backward(proj, out, d_out, seq):
    rows, width = out.shape
    group = width // IMAGES
    lanes = max(LANES, group)
    steps = width // lanes

    sums = pl.BlockSpec((8, lanes), lambda i: (0, i))
    column = pl.BlockSpec((rows, lanes), lambda i: (0, i))
    triple = pl.BlockSpec((rows, 3 * lanes), lambda i: (0, i))
    low = jax.ShapeDtypeStruct((rows, 3 * width), LOW)
    wide = jax.ShapeDtypeStruct((8, width), WIDE)
    return pl.pallas_call(
        functools.partial(attend_back_kernel, seq, group),
        grid=(steps,),
        in_specs=[triple, column, column],
        out_specs=[triple, sums, sums],
        out_shape=[low, wide, wide],
        compiler_params=pltpu.CompilerParams(vmem_limit_bytes=32 << 20),
        cost_estimate=pl.CostEstimate(
            flops=20 * rows * rows * width,
            bytes_accessed=16 * rows * width,
            transcendentals=rows * rows * width // HEAD,
        ),
    )(proj, out, d_out)


def adam_update(param, gradient, moments, decay):
    first = BETA_ONE * moments[0] + (1.0 - BETA_ONE) * gradient
    second = BETA_TWO * moments[1] + (1.0 - BETA_TWO) * gradient * gradient
    fix_one = 1.0 - BETA_ONE**STEP
    fix_two = 1.0 - BETA_TWO**STEP
    update = first / fix_one / (jnp.sqrt(second / fix_two) + ADAM_EPS) + decay * param
    return (param - LEARN_RATE * update, jnp.stack([first, second]))


def on_device(
    tokens,
    cotangent,
    image_counts,
    w_qkv,
    w_out,
    w_fc1,
    w_fc2,
    vec_small,
    fc1_bias,
    mom_qkv,
    mom_out,
    mom_fc1,
    mom_fc2,
    mom_vec,
    mom_bias,
):
    core, img, sub = lax.axis_index("core"), lax.axis_index("img"), lax.axis_index("sub")
    subs = lax.axis_size("sub")
    layers, rows = w_qkv.shape[0], w_qkv.shape[1]
    seq, feat = tokens.shape[1], tokens.shape[2]
    width = feat * IMAGES * subs
    hidden = fc1_bias.shape[1]
    padded = -(-seq // 16) * 16
    slot_live = jnp.stack([jnp.ones((), WIDE), (image_counts[0] == 2).astype(WIDE)])[:, None, None]

    inner = IMAGES * feat // 2
    kinds = (3, 1, 1, 1)
    shards = [
        w[n].reshape(rows, -1).astype(LOW)
        for n in range(layers)
        for w in (w_qkv, w_out, w_fc1, w_fc2)
    ]
    gathered = gather_weights(shards, kinds * layers)
    weights = [[gathered[4 * n + k] for k in range(4)] for n in range(layers)]

    both = jnp.concatenate(
        [
            jnp.pad(part, ((0, 0), (0, padded - seq), (0, 0)))
            for part in (tokens, (cotangent * slot_live).astype(LOW))
        ],
        axis=1,
    )
    images = to_images(both, weights[0][0])
    state, gradient = images[:padded].astype(WIDE), images[padded:]

    vec_rows = vec_small.shape[0] * vec_small.shape[1]
    small = jnp.concatenate(
        [vec_small.reshape(vec_rows, feat), fc1_bias.reshape(-1, feat)], axis=0
    )
    for bit in bits_of("sub"):
        small = gather_step(small.reshape((-1, 1) + small.shape[-2:]), "sub", bit)
    small = small.reshape((subs,) + small.shape[-2:])
    small = jnp.stack(line_in_order(small, "img"))
    vec_near = small[:, :, :vec_rows].reshape(
        (IMAGES, subs, vec_small.shape[0], vec_small.shape[1], feat)
    ).transpose(2, 3, 0, 1, 4)
    bias_near = small[:, :, vec_rows:].reshape(IMAGES, subs, layers, hidden).transpose(2, 0, 1, 3)

    def own_half(blocks_of):
        n = blocks_of.shape[-1] // 2
        lead = blocks_of.shape[:-3]
        cut = blocks_of.reshape(lead + (IMAGES, subs, 2, n))
        cut = lax.dynamic_index_in_dim(cut, sub, len(lead) + 1, keepdims=False)
        cut = lax.dynamic_index_in_dim(cut, core, len(lead) + 1, keepdims=False)
        return cut.reshape(lead + (IMAGES * n,))

    vec_half = own_half(vec_near)
    bias_half = own_half(bias_near)
    vec_full = vec_near.reshape(vec_small.shape[:2] + (width,))

    saved = []
    for n in range(layers):
        qkv_weight, out_weight, first_weight, second_weight = weights[n]
        full = vec_full[n]
        hat_one, inv_one = norm_forward(state)
        normed_one = (hat_one * full[0] + full[1]).astype(LOW)
        shift = jnp.stack([vec_half[n, 2], jnp.zeros_like(vec_half[n, 2]), vec_half[n, 3]])
        shift = shift.reshape(3, IMAGES, -1).transpose(1, 0, 2).reshape(-1)
        proj = (dot(normed_one, qkv_weight) + shift).astype(LOW)
        attended = attend_forward(proj, seq)
        middle = state + group_sum(dot(attended, out_weight, CONTRACT_LAST)) + full[4]
        hat_two, inv_two = norm_forward(middle)
        normed_two = (hat_two * full[5] + full[6]).astype(LOW)
        before = dot(normed_two, first_weight) + bias_half[n]
        active = (before * gelu_parts(before)).astype(LOW)
        branch = dot(active, second_weight, CONTRACT_LAST)
        saved.append(
            (hat_one, inv_one, normed_one, proj, attended, hat_two, inv_two, normed_two, before, active)
        )
        state = middle + group_sum(branch) + full[7]
    output = from_images(state[:seq].astype(LOW)).astype(WIDE) * slot_live

    gradient = gradient.astype(WIDE)
    big = [None] * layers
    small_grads = [None] * layers
    for n in reversed(range(layers)):
        qkv_weight, out_weight, first_weight, second_weight = weights[n]
        full = vec_full[n]
        (hat_one, inv_one, normed_one, proj, attended, hat_two, inv_two, normed_two, before, active) = saved[n]
        grad_low = gradient.astype(LOW)
        g_second = dot(grad_low, active, CONTRACT_FIRST).astype(LOW)
        g_last = jnp.sum(gradient, 0)
        slope = gelu_parts(before) + before * jnp.exp(-0.5 * before * before) * INV_ROOT_TWO_PI
        d_before = dot(grad_low, second_weight) * slope
        d_low = d_before.astype(LOW)
        if n:
            g_second, d_low = lax.optimization_barrier((g_second, d_low))
        g_bias = jnp.sum(d_before, 0)
        g_first = dot(normed_two, d_low, CONTRACT_FIRST).astype(LOW)
        d_normed = group_sum(dot(d_low, first_weight, CONTRACT_LAST))
        middle_grad, g_gain_two, g_shift_two = norm_backward(
            d_normed, hat_two, inv_two, full[5], gradient
        )
        mid_low = middle_grad.astype(LOW)
        g_out_bias = jnp.sum(middle_grad, 0)
        g_out = dot(mid_low, attended, CONTRACT_FIRST).astype(LOW)
        d_attended = dot(mid_low, out_weight).astype(LOW)
        d_proj, sum_query, sum_value = attend_backward(proj, attended, d_attended, seq)
        g_qkv = dot(normed_one, d_proj, CONTRACT_FIRST).astype(LOW)
        d_normed = group_sum(dot(d_proj, qkv_weight, CONTRACT_LAST))
        gradient, g_gain_one, g_shift_one = norm_backward(
            d_normed, hat_one, inv_one, full[0], middle_grad
        )
        big[n] = [g_second, g_first, g_out, g_qkv]
        of_features = jnp.stack(
            [g_gain_one, g_shift_one, g_out_bias, g_gain_two, g_shift_two, g_last]
        )
        small_grads[n] = jnp.concatenate(
            [of_features.reshape(-1), sum_query[0], sum_value[0], g_bias]
        ).reshape(-1, LANES)
        if n:
            big[n][0] = scatter_plain(g_second, 1)
    small_total = jnp.stack(small_grads)
    sent_back = gradient[:seq].astype(LOW)
    small_total, sent_back, big[0][-1] = lax.optimization_barrier(
        (small_total, sent_back, big[0][-1])
    )
    sent_back = from_images(sent_back)
    order = [(n, 1) for n in range(1, layers)] + [(n, 3) for n in range(1, layers)]
    order += [(0, 0), (0, 1)] + [(n, 2) for n in range(1, layers)] + [(0, 2), (0, 3)]
    summed, small_pair = scatter_grads(
        [big[n][k] for n, k in order],
        [(1, 1, 1, 3)[k] for _, k in order],
        small_total.reshape(-1, LANES),
    )
    small_pair = small_pair.reshape(2, layers, -1)
    for (n, k), total in zip(order, summed):
        big[n][k] = total
    input_grad = sent_back.astype(WIDE) * slot_live
    big = [b[::-1] for b in big]

    grads = [
        [big[n][k].reshape(w.shape[1:]) for n in range(layers)]
        for k, w in enumerate((w_qkv, w_out, w_fc1, w_fc2))
    ]

    vec_rows_of = []
    bias_rows_of = []
    for n in range(layers):
        whole = small_pair[0, n, : 6 * width].reshape(6, IMAGES, subs, feat)
        whole = lax.dynamic_index_in_dim(whole, img, 1, keepdims=False)
        whole = lax.dynamic_index_in_dim(whole, sub, 1, keepdims=False)
        split = small_pair[:, n, 6 * width : 6 * width + 2 * inner]
        split = split.reshape(2, 2, IMAGES, feat // 2)
        split = lax.dynamic_index_in_dim(split, img, 2, keepdims=False)
        fc = small_pair[:, n, 6 * width + 2 * inner :].reshape(2, IMAGES, hidden // 2)
        fc = lax.dynamic_index_in_dim(fc, img, 1, keepdims=False)
        split = jnp.where(core == 1, split[::-1], split)
        fc = jnp.where(core == 1, fc[::-1], fc)
        split = split.transpose(1, 0, 2).reshape(2, feat)
        vec_rows_of.append(
            jnp.stack(
                [whole[0], whole[1], split[0], split[1], whole[2], whole[3], whole[4], whole[5]]
            )
        )
        bias_rows_of.append(fc.reshape(-1))

    totals = tuple(jnp.stack(g) for g in grads) + (jnp.stack(vec_rows_of), jnp.stack(bias_rows_of))
    params = (w_qkv, w_out, w_fc1, w_fc2, vec_small, fc1_bias)
    moments = (mom_qkv, mom_out, mom_fc1, mom_fc2, mom_vec, mom_bias)
    decays = (WEIGHT_DECAY, WEIGHT_DECAY, WEIGHT_DECAY, WEIGHT_DECAY, 0.0, 0.0)
    results = [
        adam_update(param, total, moment, decay)
        for param, total, moment, decay in zip(params, totals, moments, decays)
    ]
    return (
        (output, input_grad)
        + totals
        + tuple(r[0] for r in results)
        + tuple(r[1] for r in results)
    )


def solution(mesh):
    dp, tensor = mesh.shape["dp"], mesh.shape["tensor"]
    inner = Mesh(
        mesh.devices.reshape(dp // 2, 2, IMAGES, tensor // IMAGES), ("pos", "core", "img", "sub")
    )
    rows, cols = ("pos", "core"), ("img", "sub")
    images = P(rows, None, cols)
    weight = [P(None, rows, None, cols)] + [P(None, rows, cols)] * 3
    moment = [P(None, None, rows, None, cols)] + [P(None, None, rows, cols)] * 3
    vector = [P(None, None, cols), P(None, cols)]
    moment_vector = [P(None, None, None, cols), P(None, None, cols)]
    return jax.shard_map(
        on_device,
        mesh=inner,
        in_specs=tuple([images, images, P(rows)] + weight + vector + moment + moment_vector),
        out_specs=tuple(
            [images, images] + weight + vector + weight + vector + moment + moment_vector
        ),
        check_vma=False,
    )
```

```python
import functools

import jax
import jax.numpy as jnp
from jax import lax
from jax.experimental import pallas as pl
from jax.experimental.pallas import tpu as pltpu
from jax.sharding import Mesh, PartitionSpec as P

HEAD = 64
STEP = 10
IMAGES = 4

NORM_EPS = 1e-06
ROOT_HALF = 0.7071067811865476
INV_ROOT_TWO_PI = 0.3989422804014327
LEARN_RATE = 0.01
BETA_ONE = 0.9
BETA_TWO = 0.999
ADAM_EPS = 1e-08
WEIGHT_DECAY = 0.05
CONTRACT_LAST = (((1,), (1,)), ((), ()))
CONTRACT_FIRST = (((0,), (0,)), ((), ()))
LOW = jnp.bfloat16
WIDE = jnp.float32
LANES = 128


def dot(left, right, dims=(((1,), (0,)), ((), ()))):
    return lax.dot_general(left, right, dims, preferred_element_type=WIDE)


def bits_of(axis):
    count = lax.axis_size(axis)
    return [1 << i for i in range(count.bit_length() - 1)]


def swap(value, axis, bit):
    count = lax.axis_size(axis)
    return lax.ppermute(value, axis, [(i, i ^ bit) for i in range(count)])


def bit_set(axis, bit):
    return (lax.axis_index(axis) // bit) % 2 == 1


def in_order(mine, arrived, axis, bit):
    upper = bit_set(axis, bit)
    return jnp.stack([jnp.where(upper, arrived, mine), jnp.where(upper, mine, arrived)])


def gather_step(mine, axis, bit):
    return in_order(mine, swap(mine, axis, bit), axis, bit)


def untangle(pieces, axis):
    for bit in bits_of(axis):
        upper = bit_set(axis, bit)
        pieces = [jnp.where(upper, pieces[d ^ bit], pieces[d]) for d in range(len(pieces))]
    return pieces


def line_in_order(value, axis):
    return untangle(
        [swap(value, axis, d) if d else value for d in range(lax.axis_size(axis))], axis
    )


MESH = pl.DeviceIdType.MESH


def greet(partners):
    barrier = pltpu.get_barrier_semaphore()
    for partner in partners:
        pl.semaphore_signal(barrier, inc=1, device_id=partner, device_id_type=MESH)
    pl.semaphore_wait(barrier, len(partners))


def partners_of(count):
    pos, img = lax.axis_index("pos"), lax.axis_index("img")
    bits = [1 << i for i in range(count.bit_length() - 1)]
    twin = [{"core": 1 - lax.axis_index("core")}]
    return twin + [{"img": img ^ d} for d in range(1, IMAGES)] + [{"pos": pos ^ b} for b in bits]


def sends_of(count):
    bits = [1 << i for i in range(count.bit_length() - 1)]
    table = []
    for which, order in enumerate((bits, bits[::-1])):
        held = [0]
        for stage, bit in enumerate(order):
            table += [(which, stage, bit, d) for d in held]
            held = held + [d | bit for d in held]
    return table


def gather_kernel(count, kinds, *refs):
    pieces = len(kinds)
    shards, wholes = refs[:pieces], refs[pieces : 2 * pieces]
    own_sem, twin_send, twin_recv, near_send, near_recv, far_send, far_recv = refs[2 * pieces :]
    pos, img, core = lax.axis_index("pos"), lax.axis_index("img"), lax.axis_index("core")
    half_rows = shards[0].shape[0]
    rows = 2 * half_rows
    table = sends_of(count)
    greet(partners_of(count))

    def place(p, q, first, blocks_wide):
        cols = shards[p].shape[1] // 2
        return wholes[p].at[
            pl.ds(pl.multiple_of(q * rows, rows), rows),
            pl.ds(pl.multiple_of(first * cols, cols), blocks_wide * cols),
        ]

    own, twin, near, far = {}, {}, {}, {}
    for p in range(pieces):
        share = shards[p].shape[1] // (2 * kinds[p])
        for k in range(kinds[p]):
            first = (img * kinds[p] + k) * share
            there = wholes[p].at[
                pl.ds(pl.multiple_of(pos * rows + core * half_rows, half_rows), half_rows),
                pl.ds(pl.multiple_of(first, share), share),
            ]

            def columns(which, p=p, k=k, share=share):
                return shards[p].at[:, pl.ds(pl.multiple_of((2 * k + which) * share, share), share)]

            twin[p, k] = pltpu.make_async_remote_copy(
                src_ref=columns(1 - core),
                dst_ref=there,
                send_sem=twin_send.at[p, k],
                recv_sem=twin_recv.at[p, k],
                device_id={"core": 1 - core},
                device_id_type=MESH,
            )
            twin[p, k].start()
            own[p, k] = pltpu.make_async_copy(columns(core), there, own_sem.at[p, k])
            own[p, k].start()

    def start_near(p):
        for k in range(kinds[p]):
            own[p, k].wait()
            twin[p, k].wait_recv()
        for d in range(1, IMAGES):
            near[p, d] = pltpu.make_async_remote_copy(
                src_ref=place(p, pos, img, 1),
                dst_ref=place(p, pos, img, 1),
                send_sem=near_send.at[p, d],
                recv_sem=near_recv.at[p, d],
                device_id={"img": img ^ d},
                device_id_type=MESH,
            )
            near[p, d].start()

    def start(p, entries):
        for e in entries:
            which, stage, bit, offset = table[e]
            there = place(p, pos ^ offset, which * (IMAGES // 2), IMAGES // 2)
            far[p, e] = pltpu.make_async_remote_copy(
                src_ref=there,
                dst_ref=there,
                send_sem=far_send.at[p, e],
                recv_sem=far_recv.at[p, e],
                device_id={"pos": pos ^ bit},
                device_id_type=MESH,
            )
            far[p, e].start()

    def forward(p):
        for e, (which, stage, bit, offset) in enumerate(table):
            if offset:
                last = max(
                    (f for f, t in enumerate(table) if t[0] == which and offset & t[2]),
                    key=lambda f: table[f][1],
                )
                source = next(
                    f
                    for f, t in enumerate(table)
                    if t[0] == which and t[2] == table[last][2] and t[3] == offset ^ table[last][2]
                )
                if (p, source) not in landed:
                    far[p, source].wait_recv()
                    landed.add((p, source))
                start(p, [e])

    landed = set()
    for p in range(min(AHEAD, pieces)):
        start_near(p)
    for p in range(pieces):
        if p + AHEAD < pieces:
            start_near(p + AHEAD)
        for d in range(1, IMAGES):
            near[p, d].wait_recv()
        start(p, [e for e, t in enumerate(table) if t[3] == 0])
        if p:
            forward(p - 1)
    forward(pieces - 1)
    for p in range(pieces):
        for k in range(kinds[p]):
            twin[p, k].wait_send()
        for d in range(1, IMAGES):
            near[p, d].wait_send()
        for e in range(len(table)):
            if (p, e) not in landed:
                far[p, e].wait_recv()
            far[p, e].wait_send()


def cut_halves(shard, kinds):
    pair = shard.reshape(shard.shape[0], kinds, 2, -1)
    return [pair[:, :, which].reshape(shard.shape[0], -1) for which in range(2)]


def gather_plain(shard, kinds):
    core = lax.axis_index("core")
    pair = cut_halves(shard, kinds)
    kept = jnp.where(core == 1, pair[1], pair[0])
    sent = jnp.where(core == 1, pair[0], pair[1])
    block = in_order(kept, swap(sent, "core", 1), "core", 1).reshape(2 * shard.shape[0], -1)
    whole = lax.all_gather(block, ("img", "pos")).reshape(IMAGES, -1, block.shape[1])
    return jnp.concatenate([whole[i] for i in range(IMAGES)], axis=1)


def scatter_plain(grad, kinds):
    core, count = lax.axis_index("core"), lax.axis_size("pos")
    parts = jnp.stack(jnp.split(grad, IMAGES, axis=1))
    parts = parts.reshape(IMAGES * count, grad.shape[0] // count, -1)
    block = lax.psum_scatter(parts, ("img", "pos")).astype(WIDE)
    block = block.reshape(2, block.shape[0] // 2, -1)
    kept = jnp.where(core == 1, block[1], block[0])
    sent = jnp.where(core == 1, block[0], block[1]).astype(LOW)
    both = in_order(kept, swap(sent, "core", 1).astype(WIDE), "core", 1)
    both = both.reshape(2, both.shape[1], kinds, -1).transpose(1, 2, 0, 3)
    return both.reshape(both.shape[0], -1)


def aligned(width, kinds):
    return width // (2 * kinds) % LANES == 0


def gather_weights(shards, kinds):
    if not all(aligned(w.shape[1], k) for w, k in zip(shards, kinds)):
        good = [i for i, w in enumerate(shards) if aligned(w.shape[1], kinds[i])]
        done = dict(zip(good, gather_weights([shards[i] for i in good], [kinds[i] for i in good])))
        return [
            done[i] if i in done else gather_plain(w, kinds[i]) for i, w in enumerate(shards)
        ]
    count, pieces = lax.axis_size("pos"), len(shards)
    copies, most = len(sends_of(count)), max(kinds)
    moved = sum(2 * count * IMAGES * w.size for w in shards)
    anywhere = pl.BlockSpec(memory_space=pl.ANY)
    return pl.pallas_call(
        functools.partial(gather_kernel, count, tuple(kinds)),
        in_specs=[anywhere] * pieces,
        out_specs=[anywhere] * pieces,
        out_shape=[
            jax.ShapeDtypeStruct((count * 2 * w.shape[0], IMAGES * w.shape[1] // 2), LOW)
            for w in shards
        ],
        scratch_shapes=[
            pltpu.SemaphoreType.DMA((pieces, most)),
            pltpu.SemaphoreType.DMA((pieces, most)),
            pltpu.SemaphoreType.DMA((pieces, most)),
            pltpu.SemaphoreType.DMA((pieces, IMAGES)),
            pltpu.SemaphoreType.DMA((pieces, IMAGES)),
            pltpu.SemaphoreType.DMA((pieces, copies)),
            pltpu.SemaphoreType.DMA((pieces, copies)),
        ],
        compiler_params=pltpu.CompilerParams(collective_id=0, has_side_effects=True),
        cost_estimate=pl.CostEstimate(flops=0, bytes_accessed=8 * moved, transcendentals=0),
    )(*shards)


def receipts_of(count):
    bits = [1 << i for i in range(count.bit_length() - 1)]
    table = []
    for which, order in enumerate((bits[::-1], bits)):
        kept = list(range(count))
        for stage, bit in enumerate(order):
            kept = [d for d in kept if not d & bit]
            table += [(which, stage, bit, d) for d in kept]
    return table


CHUNK = 64
AHEAD = 1


def scatter_kernel(count, kinds, *refs):
    pieces = len(kinds)
    grads, small, refs = refs[:pieces], refs[pieces], refs[pieces + 1 :]
    outs, small_out, refs = refs[:pieces], refs[pieces], refs[pieces + 1 :]
    arrived, sums, near, gone, come = [refs[i * pieces : (i + 1) * pieces] for i in range(5)]
    far_send, far_recv, near_send, near_recv, twin_send, twin_recv = refs[5 * pieces : -4]
    small_sum, small_in, small_send, small_recv = refs[-4:]
    pos, img, core = lax.axis_index("pos"), lax.axis_index("img"), lax.axis_index("core")
    half_rows = outs[0].shape[0]
    rows = 2 * half_rows
    table = receipts_of(count)
    stages = max(t[1] for t in table) + 1
    half = IMAGES // 2
    greet(partners_of(count))
    far, close, twin = {}, {}, {}

    partial = {}

    def whole_part(p, which, offset):
        cols = outs[p].shape[1] // 2
        return grads[p].at[
            pl.ds(pl.multiple_of((pos ^ offset) * rows, rows), rows),
            pl.ds(which * half * cols, half * cols),
        ]

    def send(p, stage):
        for e, (which, at, bit, offset) in enumerate(table):
            if at == stage:
                far[p, e] = pltpu.make_async_remote_copy(
                    src_ref=partial[p, which, offset | bit]
                    if stage
                    else whole_part(p, which, offset | bit),
                    dst_ref=arrived[p].at[e],
                    send_sem=far_send.at[p, e],
                    recv_sem=far_recv.at[p, e],
                    device_id={"pos": pos ^ bit},
                    device_id_type=MESH,
                )
                far[p, e].start()

    def add(p, stage):
        for e, (which, at, bit, offset) in enumerate(table):
            if at != stage:
                continue
            far[p, e].wait_recv()
            cols = outs[p].shape[1] // 2
            before = partial[p, which, offset] if stage else whole_part(p, which, offset)
            slot = arrived[p].at[e]

            def body(i, carry, before=before, slot=slot, which=which, p=p, cols=cols):
                step = pl.ds(pl.multiple_of(i * CHUNK, CHUNK), CHUNK)
                total = (before[step, :].astype(WIDE) + slot[step, :].astype(WIDE)).astype(LOW)
                if stage < stages - 1:
                    slot[step, :] = total
                else:
                    for j in range(half):
                        sums[p][which * half + j, step] = total[:, j * cols : (j + 1) * cols]
                return carry

            lax.fori_loop(0, rows // CHUNK, body, 0)
            partial[p, which, offset] = slot

    def send_near(p):
        for d in range(1, IMAGES):
            close[p, d] = pltpu.make_async_remote_copy(
                src_ref=sums[p].at[img ^ d],
                dst_ref=near[p].at[d - 1],
                send_sem=near_send.at[p, d],
                recv_sem=near_recv.at[p, d],
                device_id={"img": img ^ d},
                device_id_type=MESH,
            )
            close[p, d].start()

    def columns(p, k, which):
        share = outs[p].shape[1] // (2 * kinds[p])
        return pl.ds(pl.multiple_of((2 * k + which) * share, share), share)

    def finish(p):
        share = outs[p].shape[1] // (2 * kinds[p])
        for d in range(1, IMAGES):
            close[p, d].wait_recv()

        def total_of(first):
            step = pl.ds(pl.multiple_of(first, CHUNK), CHUNK)
            total = sums[p][img, step].astype(WIDE)
            for d in range(1, IMAGES):
                total += near[p][d - 1, step].astype(WIDE)
            return total

        def other(i, carry):
            step = pl.ds(pl.multiple_of(i * CHUNK, CHUNK), CHUNK)
            gone[p][step, :] = total_of((1 - core) * half_rows + i * CHUNK).astype(LOW)
            return carry

        lax.fori_loop(0, half_rows // CHUNK, other, 0)
        twin[p] = pltpu.make_async_remote_copy(
            src_ref=gone[p],
            dst_ref=come[p],
            send_sem=twin_send.at[p],
            recv_sem=twin_recv.at[p],
            device_id={"core": 1 - core},
            device_id_type=MESH,
        )
        twin[p].start()

        def mine(i, carry):
            step = pl.ds(pl.multiple_of(i * CHUNK, CHUNK), CHUNK)
            total = total_of(core * half_rows + i * CHUNK)
            for k in range(kinds[p]):
                outs[p][step, columns(p, k, core)] = total[:, k * share : (k + 1) * share]
            return carry

        lax.fori_loop(0, half_rows // CHUNK, mine, 0)

    def close_twin(p):
        share = outs[p].shape[1] // (2 * kinds[p])
        twin[p].wait_recv()

        def body(i, carry):
            step = pl.ds(pl.multiple_of(i * CHUNK, CHUNK), CHUNK)
            total = come[p][step, :].astype(WIDE)
            for k in range(kinds[p]):
                outs[p][step, columns(p, k, 1 - core)] = total[:, k * share : (k + 1) * share]
            return carry

        lax.fori_loop(0, half_rows // CHUNK, body, 0)

    steps = [("img", 1), ("img", 2)] + [("pos", 1 << i) for i in range(stages)] + [("core", 1)]
    passed = {}

    def small_step(turn):
        if 0 < turn <= len(steps):
            passed[turn - 1].wait_recv()
        if turn < len(steps):
            before = small if turn == 0 else small_sum.at[turn - 1]
            small_sum[turn] = small[...] if turn == 0 else before[...] + small_in[turn - 1]
            axis, bit = steps[turn]
            passed[turn] = pltpu.make_async_remote_copy(
                src_ref=small_sum.at[turn],
                dst_ref=small_in.at[turn],
                send_sem=small_send.at[turn],
                recv_sem=small_recv.at[turn],
                device_id={axis: lax.axis_index(axis) ^ bit},
                device_id_type=MESH,
            )
            passed[turn].start()
        if turn == len(steps):
            small_out[0] = small_sum[turn - 1]
            small_out[1] = small_in[turn - 1]

    turns = max(pieces + stages + 2, len(steps) + 1)
    for turn in range(turns):
        if turn < pieces:
            send(turn, 0)
        small_step(turn)
        for stage in range(stages):
            p = turn - 1 - stage
            if 0 <= p < pieces:
                add(p, stage)
                if stage < stages - 1:
                    send(p, stage + 1)
                else:
                    send_near(p)
        p = turn - 1 - stages
        if 0 <= p < pieces:
            finish(p)
        p -= 1
        if 0 <= p < pieces:
            close_twin(p)
    for turn in range(len(steps)):
        passed[turn].wait_send()
    for p in range(pieces):
        twin[p].wait_send()
        for e in range(len(table)):
            far[p, e].wait_send()
        for d in range(1, IMAGES):
            close[p, d].wait_send()


def scatter_grads(grads, kinds, small):
    widths = [2 * g.shape[1] // IMAGES for g in grads]
    if not all(aligned(w, k) for w, k in zip(widths, kinds)):
        good = [i for i, w in enumerate(widths) if aligned(w, kinds[i])]
        summed, small = scatter_grads([grads[i] for i in good], [kinds[i] for i in good], small)
        done = dict(zip(good, summed))
        every = [done[i] if i in done else scatter_plain(g, kinds[i]) for i, g in enumerate(grads)]
        return every, small
    count, pieces = lax.axis_size("pos"), len(grads)
    copies = len(receipts_of(count))
    shapes = [(g.shape[0] // count, g.shape[1] // IMAGES) for g in grads]
    in_vmem = pl.BlockSpec(memory_space=pltpu.VMEM)
    moved = sum(2 * g.size for g in grads)
    steps = count.bit_length() - 1 + 3
    out = pl.pallas_call(
        functools.partial(scatter_kernel, count, tuple(kinds)),
        in_specs=[in_vmem] * (pieces + 1),
        out_specs=[in_vmem] * (pieces + 1),
        out_shape=[jax.ShapeDtypeStruct((r // 2, 2 * c), WIDE) for r, c in shapes]
        + [jax.ShapeDtypeStruct((2,) + small.shape, WIDE)],
        scratch_shapes=[pltpu.VMEM((copies, r, IMAGES // 2 * c), LOW) for r, c in shapes]
        + [pltpu.VMEM((IMAGES, r, c), LOW) for r, c in shapes]
        + [pltpu.VMEM((IMAGES - 1, r, c), LOW) for r, c in shapes]
        + [pltpu.VMEM((r // 2, c), LOW) for r, c in shapes]
        + [pltpu.VMEM((r // 2, c), LOW) for r, c in shapes]
        + [
            pltpu.SemaphoreType.DMA((pieces, copies)),
            pltpu.SemaphoreType.DMA((pieces, copies)),
            pltpu.SemaphoreType.DMA((pieces, IMAGES)),
            pltpu.SemaphoreType.DMA((pieces, IMAGES)),
            pltpu.SemaphoreType.DMA((pieces,)),
            pltpu.SemaphoreType.DMA((pieces,)),
            pltpu.VMEM((steps,) + small.shape, WIDE),
            pltpu.VMEM((steps,) + small.shape, WIDE),
            pltpu.SemaphoreType.DMA((steps,)),
            pltpu.SemaphoreType.DMA((steps,)),
        ],
        compiler_params=pltpu.CompilerParams(
            collective_id=1, has_side_effects=True, vmem_limit_bytes=48 << 20
        ),
        cost_estimate=pl.CostEstimate(flops=0, bytes_accessed=8 * moved, transcendentals=0),
    )(*grads, small)
    return list(out[:-1]), out[-1]


def group_sum(partial):
    for axis in ("core", "sub"):
        for bit in bits_of(axis):
            partial = partial + swap(partial.astype(LOW), axis, bit).astype(WIDE)
    return partial


def send_column(value, distance):
    return lax.ppermute(value, ("core", "img"), distance)


def to_images(slots, after):
    core, img = lax.axis_index("core"), lax.axis_index("img")
    pieces = []
    for distance in range(IMAGES):
        payload = jnp.where((img ^ distance) % 2 == 1, slots[1], slots[0])
        if distance:
            pairs = [
                (c * IMAGES + (i ^ distance), c * IMAGES + i)
                for c in range(2)
                for i in range(IMAGES)
                if i // 2 == c
            ]
            payload = send_column(payload, pairs)
        pieces.append(payload)
    pieces, after = lax.optimization_barrier((pieces, after))
    pieces = untangle(pieces, "img")
    for bit in bits_of("sub"):
        pieces = [
            jnp.concatenate(list(gather_step(p, "sub", bit)), axis=-1) for p in pieces
        ]
    mine = jnp.concatenate(pieces, axis=-1)
    return jnp.where(img // 2 == core, mine, swap(mine, "core", 1))


def from_images(image):
    core, img, sub = lax.axis_index("core"), lax.axis_index("img"), lax.axis_index("sub")
    seq, width = image.shape
    subs = lax.axis_size("sub")
    share = width // (IMAGES * subs)
    image = image.reshape(seq, IMAGES, subs, share)
    if subs > 1:
        image = lax.dynamic_index_in_dim(image, sub, 2, keepdims=True)
    blocks = [image[:, i, 0] for i in range(IMAGES)]
    blocks = untangle(blocks, "img")
    pieces = [blocks[0]]
    for distance in range(1, IMAGES):
        pairs = [
            (c * IMAGES + i, c * IMAGES + (i ^ distance))
            for c in range(2)
            for i in range(IMAGES)
            if i // 2 == c
        ]
        pieces.append(send_column(blocks[distance], pairs))
    pieces = untangle(pieces, "img")
    return jnp.stack([jnp.where(core == 1, pieces[2 + s], pieces[s]) for s in range(2)])


def gelu_parts(value):
    return 0.5 * (1.0 + lax.erf(value * ROOT_HALF))


def norm_forward(hidden):
    mean = jnp.mean(hidden, -1, keepdims=True)
    spread = jnp.mean(hidden * hidden, -1, keepdims=True) - mean * mean
    inv = lax.rsqrt(spread + NORM_EPS)
    return (hidden - mean) * inv, inv


def norm_backward(d_normed, normed, inv, gain, carried):
    d_hat = d_normed * gain
    plain = jnp.mean(d_hat, -1, keepdims=True)
    crossed = jnp.mean(d_hat * normed, -1, keepdims=True)
    grad = carried + inv * (d_hat - plain - normed * crossed)
    return grad, jnp.sum(d_normed * normed, 0), jnp.sum(d_normed, 0)


def softmax_rows(query, key, seq):
    scores = dot(query, key, CONTRACT_LAST) * HEAD ** (-0.5)
    column = lax.broadcasted_iota(jnp.int32, scores.shape, 1)
    scores = jnp.where(column < seq, scores, -1e30)
    raised = jnp.exp(scores - jnp.max(scores, -1, keepdims=True))
    return raised * (1.0 / jnp.sum(raised, -1, keepdims=True))


def split_three(value, group):
    cuts = [value[:, i : i + group] for i in range(0, value.shape[1], group)]
    if len(cuts) == 3:
        return cuts
    return [jnp.concatenate(cuts[k::3], axis=1) for k in range(3)]


def attend_kernel(seq, group, proj_ref, o_ref):
    query, key, value = split_three(proj_ref[...], group)
    lane_head = lax.broadcasted_iota(jnp.int32, query.shape, 1) // HEAD
    total = jnp.zeros(query.shape, WIDE)
    for head in range(query.shape[1] // HEAD):
        own = lane_head == head
        probs = softmax_rows(jnp.where(own, query, jnp.zeros_like(query)), key, seq)
        total = jnp.where(own, dot(probs.astype(LOW), value), total)
    o_ref[...] = total.astype(LOW)


def attend_back_kernel(seq, group, proj_ref, o_ref, do_ref, dproj_ref, sq_ref, sv_ref):
    query, key, value = split_three(proj_ref[...], group)
    out, d_out = o_ref[...].astype(WIDE), do_ref[...]
    lane_head = lax.broadcasted_iota(jnp.int32, query.shape, 1) // HEAD
    d_query = jnp.zeros(query.shape, WIDE)
    d_key = jnp.zeros(query.shape, WIDE)
    d_value = jnp.zeros(query.shape, WIDE)
    for head in range(query.shape[1] // HEAD):
        own = lane_head == head
        probs = softmax_rows(jnp.where(own, query, jnp.zeros_like(query)), key, seq)
        d_own = jnp.where(own, d_out, jnp.zeros_like(d_out))
        d_value = jnp.where(own, dot(probs.astype(LOW), d_out, CONTRACT_FIRST), d_value)
        d_probs = dot(d_own, value, CONTRACT_LAST)
        delta = jnp.sum(d_own.astype(WIDE) * out, -1, keepdims=True)
        d_scores = (probs * (d_probs - delta) * HEAD ** (-0.5)).astype(LOW)
        d_query = jnp.where(own, dot(d_scores, key), d_query)
        d_key = jnp.where(own, dot(d_scores, query, CONTRACT_FIRST), d_key)
    for which, part in enumerate((d_query, d_key, d_value)):
        for j in range(part.shape[1] // group):
            at = (3 * j + which) * group
            dproj_ref[:, at : at + group] = part[:, j * group : (j + 1) * group].astype(LOW)
    sq_ref[...] = jnp.broadcast_to(jnp.sum(d_query, 0, keepdims=True), sq_ref.shape)
    sv_ref[...] = jnp.broadcast_to(jnp.sum(d_value, 0, keepdims=True), sv_ref.shape)


def attend_forward(proj, seq):
    rows, width = proj.shape[0], proj.shape[1] // 3
    group = width // IMAGES
    lanes = max(LANES, group)
    steps = width // lanes

    return pl.pallas_call(
        functools.partial(attend_kernel, seq, group),
        grid=(steps,),
        in_specs=[pl.BlockSpec((rows, 3 * lanes), lambda i: (0, i))],
        out_specs=pl.BlockSpec((rows, lanes), lambda i: (0, i)),
        out_shape=jax.ShapeDtypeStruct((rows, width), LOW),
        compiler_params=pltpu.CompilerParams(vmem_limit_bytes=32 << 20),
        cost_estimate=pl.CostEstimate(
            flops=8 * rows * rows * width,
            bytes_accessed=8 * rows * width,
            transcendentals=rows * rows * width // HEAD,
        ),
    )(proj)


def attend_backward(proj, out, d_out, seq):
    rows, width = out.shape
    group = width // IMAGES
    lanes = max(LANES, group)
    steps = width // lanes

    sums = pl.BlockSpec((8, lanes), lambda i: (0, i))
    column = pl.BlockSpec((rows, lanes), lambda i: (0, i))
    triple = pl.BlockSpec((rows, 3 * lanes), lambda i: (0, i))
    low = jax.ShapeDtypeStruct((rows, 3 * width), LOW)
    wide = jax.ShapeDtypeStruct((8, width), WIDE)
    return pl.pallas_call(
        functools.partial(attend_back_kernel, seq, group),
        grid=(steps,),
        in_specs=[triple, column, column],
        out_specs=[triple, sums, sums],
        out_shape=[low, wide, wide],
        compiler_params=pltpu.CompilerParams(vmem_limit_bytes=32 << 20),
        cost_estimate=pl.CostEstimate(
            flops=20 * rows * rows * width,
            bytes_accessed=16 * rows * width,
            transcendentals=rows * rows * width // HEAD,
        ),
    )(proj, out, d_out)


def adam_update(param, gradient, moments, decay):
    first = BETA_ONE * moments[0] + (1.0 - BETA_ONE) * gradient
    second = BETA_TWO * moments[1] + (1.0 - BETA_TWO) * gradient * gradient
    fix_one = 1.0 - BETA_ONE**STEP
    fix_two = 1.0 - BETA_TWO**STEP
    update = first / fix_one / (jnp.sqrt(second / fix_two) + ADAM_EPS) + decay * param
    return (param - LEARN_RATE * update, jnp.stack([first, second]))


def on_device(
    tokens,
    cotangent,
    image_counts,
    w_qkv,
    w_out,
    w_fc1,
    w_fc2,
    vec_small,
    fc1_bias,
    mom_qkv,
    mom_out,
    mom_fc1,
    mom_fc2,
    mom_vec,
    mom_bias,
):
    core, img, sub = lax.axis_index("core"), lax.axis_index("img"), lax.axis_index("sub")
    subs = lax.axis_size("sub")
    layers, rows = w_qkv.shape[0], w_qkv.shape[1]
    seq, feat = tokens.shape[1], tokens.shape[2]
    width = feat * IMAGES * subs
    hidden = fc1_bias.shape[1]
    padded = -(-seq // 16) * 16
    slot_live = jnp.stack([jnp.ones((), WIDE), (image_counts[0] == 2).astype(WIDE)])[:, None, None]

    inner = IMAGES * feat // 2
    kinds = (3, 1, 1, 1)
    shards = [
        w[n].reshape(rows, -1).astype(LOW)
        for n in range(layers)
        for w in (w_qkv, w_out, w_fc1, w_fc2)
    ]
    gathered = gather_weights(shards, kinds * layers)
    weights = [[gathered[4 * n + k] for k in range(4)] for n in range(layers)]

    both = jnp.concatenate(
        [
            jnp.pad(part, ((0, 0), (0, padded - seq), (0, 0)))
            for part in (tokens, (cotangent * slot_live).astype(LOW))
        ],
        axis=1,
    )
    images = to_images(both, weights[0][0])
    state, gradient = images[:padded].astype(WIDE), images[padded:]

    vec_rows = vec_small.shape[0] * vec_small.shape[1]
    small = jnp.concatenate(
        [vec_small.reshape(vec_rows, feat), fc1_bias.reshape(-1, feat)], axis=0
    )
    for bit in bits_of("sub"):
        small = gather_step(small.reshape((-1, 1) + small.shape[-2:]), "sub", bit)
    small = small.reshape((subs,) + small.shape[-2:])
    small = jnp.stack(line_in_order(small, "img"))
    vec_near = small[:, :, :vec_rows].reshape(
        (IMAGES, subs, vec_small.shape[0], vec_small.shape[1], feat)
    ).transpose(2, 3, 0, 1, 4)
    bias_near = small[:, :, vec_rows:].reshape(IMAGES, subs, layers, hidden).transpose(2, 0, 1, 3)

    def own_half(blocks_of):
        n = blocks_of.shape[-1] // 2
        lead = blocks_of.shape[:-3]
        cut = blocks_of.reshape(lead + (IMAGES, subs, 2, n))
        cut = lax.dynamic_index_in_dim(cut, sub, len(lead) + 1, keepdims=False)
        cut = lax.dynamic_index_in_dim(cut, core, len(lead) + 1, keepdims=False)
        return cut.reshape(lead + (IMAGES * n,))

    vec_half = own_half(vec_near)
    bias_half = own_half(bias_near)
    vec_full = vec_near.reshape(vec_small.shape[:2] + (width,))

    saved = []
    for n in range(layers):
        qkv_weight, out_weight, first_weight, second_weight = weights[n]
        full = vec_full[n]
        hat_one, inv_one = norm_forward(state)
        normed_one = (hat_one * full[0] + full[1]).astype(LOW)
        shift = jnp.stack([vec_half[n, 2], jnp.zeros_like(vec_half[n, 2]), vec_half[n, 3]])
        shift = shift.reshape(3, IMAGES, -1).transpose(1, 0, 2).reshape(-1)
        proj = (dot(normed_one, qkv_weight) + shift).astype(LOW)
        attended = attend_forward(proj, seq)
        middle = state + group_sum(dot(attended, out_weight, CONTRACT_LAST)) + full[4]
        hat_two, inv_two = norm_forward(middle)
        normed_two = (hat_two * full[5] + full[6]).astype(LOW)
        before = dot(normed_two, first_weight) + bias_half[n]
        active = (before * gelu_parts(before)).astype(LOW)
        branch = dot(active, second_weight, CONTRACT_LAST)
        saved.append(
            (hat_one, inv_one, normed_one, proj, attended, hat_two, inv_two, normed_two, before, active)
        )
        state = middle + group_sum(branch) + full[7]
    output = from_images(state[:seq].astype(LOW)).astype(WIDE) * slot_live

    gradient = gradient.astype(WIDE)
    big = [None] * layers
    small_grads = [None] * layers
    for n in reversed(range(layers)):
        qkv_weight, out_weight, first_weight, second_weight = weights[n]
        full = vec_full[n]
        (hat_one, inv_one, normed_one, proj, attended, hat_two, inv_two, normed_two, before, active) = saved[n]
        grad_low = gradient.astype(LOW)
        g_second = dot(grad_low, active, CONTRACT_FIRST).astype(LOW)
        g_last = jnp.sum(gradient, 0)
        slope = gelu_parts(before) + before * jnp.exp(-0.5 * before * before) * INV_ROOT_TWO_PI
        d_before = dot(grad_low, second_weight) * slope
        d_low = d_before.astype(LOW)
        if n:
            g_second, d_low = lax.optimization_barrier((g_second, d_low))
        g_bias = jnp.sum(d_before, 0)
        g_first = dot(normed_two, d_low, CONTRACT_FIRST).astype(LOW)
        d_normed = group_sum(dot(d_low, first_weight, CONTRACT_LAST))
        middle_grad, g_gain_two, g_shift_two = norm_backward(
            d_normed, hat_two, inv_two, full[5], gradient
        )
        mid_low = middle_grad.astype(LOW)
        g_out_bias = jnp.sum(middle_grad, 0)
        g_out = dot(mid_low, attended, CONTRACT_FIRST).astype(LOW)
        d_attended = dot(mid_low, out_weight).astype(LOW)
        d_proj, sum_query, sum_value = attend_backward(proj, attended, d_attended, seq)
        g_qkv = dot(normed_one, d_proj, CONTRACT_FIRST).astype(LOW)
        d_normed = group_sum(dot(d_proj, qkv_weight, CONTRACT_LAST))
        gradient, g_gain_one, g_shift_one = norm_backward(
            d_normed, hat_one, inv_one, full[0], middle_grad
        )
        big[n] = [g_second, g_first, g_out, g_qkv]
        of_features = jnp.stack(
            [g_gain_one, g_shift_one, g_out_bias, g_gain_two, g_shift_two, g_last]
        )
        small_grads[n] = jnp.concatenate(
            [of_features.reshape(-1), sum_query[0], sum_value[0], g_bias]
        ).reshape(-1, LANES)
        if n:
            big[n][0] = scatter_plain(g_second, 1)
    small_total = jnp.stack(small_grads)
    sent_back = gradient[:seq].astype(LOW)
    small_total, sent_back, big[0][-1] = lax.optimization_barrier(
        (small_total, sent_back, big[0][-1])
    )
    sent_back = from_images(sent_back)
    order = [(n, 1) for n in range(1, layers)] + [(n, 3) for n in range(1, layers)]
    order += [(0, 0), (0, 1)] + [(n, 2) for n in range(1, layers)] + [(0, 2), (0, 3)]
    summed, small_pair = scatter_grads(
        [big[n][k] for n, k in order],
        [(1, 1, 1, 3)[k] for _, k in order],
        small_total.reshape(-1, LANES),
    )
    small_pair = small_pair.reshape(2, layers, -1)
    for (n, k), total in zip(order, summed):
        big[n][k] = total
    input_grad = sent_back.astype(WIDE) * slot_live
    big = [b[::-1] for b in big]

    grads = [
        [big[n][k].reshape(w.shape[1:]) for n in range(layers)]
        for k, w in enumerate((w_qkv, w_out, w_fc1, w_fc2))
    ]

    vec_rows_of = []
    bias_rows_of = []
    for n in range(layers):
        whole = small_pair[0, n, : 6 * width].reshape(6, IMAGES, subs, feat)
        whole = lax.dynamic_index_in_dim(whole, img, 1, keepdims=False)
        whole = lax.dynamic_index_in_dim(whole, sub, 1, keepdims=False)
        split = small_pair[:, n, 6 * width : 6 * width + 2 * inner]
        split = split.reshape(2, 2, IMAGES, feat // 2)
        split = lax.dynamic_index_in_dim(split, img, 2, keepdims=False)
        fc = small_pair[:, n, 6 * width + 2 * inner :].reshape(2, IMAGES, hidden // 2)
        fc = lax.dynamic_index_in_dim(fc, img, 1, keepdims=False)
        split = jnp.where(core == 1, split[::-1], split)
        fc = jnp.where(core == 1, fc[::-1], fc)
        split = split.transpose(1, 0, 2).reshape(2, feat)
        vec_rows_of.append(
            jnp.stack(
                [whole[0], whole[1], split[0], split[1], whole[2], whole[3], whole[4], whole[5]]
            )
        )
        bias_rows_of.append(fc.reshape(-1))

    totals = tuple(jnp.stack(g) for g in grads) + (jnp.stack(vec_rows_of), jnp.stack(bias_rows_of))
    params = (w_qkv, w_out, w_fc1, w_fc2, vec_small, fc1_bias)
    moments = (mom_qkv, mom_out, mom_fc1, mom_fc2, mom_vec, mom_bias)
    decays = (WEIGHT_DECAY, WEIGHT_DECAY, WEIGHT_DECAY, WEIGHT_DECAY, 0.0, 0.0)
    results = [
        adam_update(param, total, moment, decay)
        for param, total, moment, decay in zip(params, totals, moments, decays)
    ]
    return (
        (output, input_grad)
        + totals
        + tuple(r[0] for r in results)
        + tuple(r[1] for r in results)
    )


def solution(mesh):
    dp, tensor = mesh.shape["dp"], mesh.shape["tensor"]
    inner = Mesh(
        mesh.devices.reshape(dp // 2, 2, IMAGES, tensor // IMAGES), ("pos", "core", "img", "sub")
    )
    rows, cols = ("pos", "core"), ("img", "sub")
    images = P(rows, None, cols)
    weight = [P(None, rows, None, cols)] + [P(None, rows, cols)] * 3
    moment = [P(None, None, rows, None, cols)] + [P(None, None, rows, cols)] * 3
    vector = [P(None, None, cols), P(None, cols)]
    moment_vector = [P(None, None, None, cols), P(None, None, cols)]
    return jax.shard_map(
        on_device,
        mesh=inner,
        in_specs=tuple([images, images, P(rows)] + weight + vector + moment + moment_vector),
        out_specs=tuple(
            [images, images] + weight + vector + weight + vector + moment + moment_vector
        ),
        check_vma=False,
    )
```
